256 devices in a mesh: gx: 16 (over y_hi, x, core), gy: 8 (over z), gz: 2 (over y_lo).
Axes of the slice: x: 4, y: 4 (y_hi: 2, y_lo: 2; y = y_hi * 2 + y_lo), z: 8, core: 2. Of those that a mesh axis runs over, the one named last changes fastest.
Arguments:
- e_forward: float32 [3, 256, 256, 256], P(None, 'gx', 'gy', 'gz'), may hold values from -6 to 6
- h_forward: float32 [3, 256, 256, 256], P(None, 'gx', 'gy', 'gz'), may hold values from -6 to 6
- e_adjoint: float32 [3, 256, 256, 256], P(None, 'gx', 'gy', 'gz'), may hold values from -6 to 6
- h_adjoint: float32 [3, 256, 256, 256], P(None, 'gx', 'gy', 'gz'), may hold values from -6 to 6
- material: int32 [256, 256, 256], P('gx', 'gy', 'gz'), may hold values from 0 to 3
- dft_forward: float32 [3, 2, 3, 96, 256, 256], P(None, None, None, 'gz', 'gx', 'gy'), may hold values from -6 to 6
- dft_adjoint: float32 [3, 2, 3, 96, 256, 256], P(None, None, None, 'gz', 'gx', 'gy'), may hold values from -6 to 6
- angular_freq: float32 [3], replicated, may hold values from 0.05 to 0.6
- layer_map: int32 [96], replicated, may hold values from 0 to 15, as said below
Outputs:
- e_forward_new: float32 [3, 256, 256, 256], P(None, 'gx', 'gy', 'gz')
- h_forward_new: float32 [3, 256, 256, 256], P(None, 'gx', 'gy', 'gz')
- e_adjoint_new: float32 [3, 256, 256, 256], P(None, 'gx', 'gy', 'gz')
- h_adjoint_new: float32 [3, 256, 256, 256], P(None, 'gx', 'gy', 'gz')
- gradient: float32 [16, 256, 256], P('gz', 'gx', 'gy')
The draws below stay inside these ranges and needn't reach their ends.
Inputs may be any that keep to these rules, and one draw needn't show every extreme that they name: `layer_map`: every design layer owns one contiguous nonempty run of the 96 slab cells; the runs' order along the slab is arbitrary.
All inputs are finite; a program needn't handle non-finite values.
Results may differ from the reference program's by a relative error of at most 0.000073.
Values sent between devices are 32-bit elements; how exact they have to be, the bound alone decides.
A program may use at most 128 MiB of HBM per device.

```python
import math
import jax
import jax.numpy as jnp
from jax import lax

SLAB = 96
LAYERS = 16
FREQS = 3
STEP = 40
NX = 256
NY = 256
NZ = 256


def draw_layer_map(key, part):
    first_key, second_key = jax.random.split(jax.random.fold_in(key, 11))
    picks = jax.random.permutation(first_key, SLAB - 1)[:LAYERS - 1] + 1
    cuts = jnp.sort(picks)
    run_number = jnp.sum(jnp.arange(SLAB)[:, None] >= cuts[None, :], axis=1)
    ordering = jax.random.permutation(second_key, LAYERS)
    return ordering[run_number].astype(jnp.int32)


def place_ends(array, rng, least, top_value):
    longest = array.shape.index(max(array.shape))
    spots = []
    for shift in (0, 1):
        where = [jax.random.randint(jax.random.fold_in(rng, axis), (), 0, length) for axis, length in enumerate(array.shape)]
        where[longest] = (where[longest] + shift) % array.shape[longest]
        spots.append(tuple(where))
    return array.at[spots[0]].set(least).at[spots[1]].set(top_value)


def block_levels(rng, dims, cuts, low, largest):
    loudness, own = 1.0, jax.random.fold_in(rng, 6)
    for position, shards_of in cuts:
        draws = jnp.exp(jax.random.uniform(jax.random.fold_in(own, position), (shards_of,), jnp.float32, low / len(cuts), largest / len(cuts)))
        loudness = loudness * jnp.repeat(draws, dims[position] // shards_of).reshape([-1 if axis == position else 1 for axis in range(len(dims))])
    return loudness


def noise(own_key, dims, scale, most, cuts=(), kind=jnp.bfloat16):
    drawn = jax.random.normal(own_key, dims, jnp.float32) * scale
    if len(cuts) > 0:
        drawn = block_levels(own_key, dims, cuts, -0.22, 0.18) * drawn
    return jnp.clip(drawn, min=-most, max=most).astype(kind)


def setup_inputs(seed: int = 0) -> dict:
    key_of = jax.random.split(jax.random.key(seed), 10)
    e_forward = noise(key_of[0], (3, NX, NY, NZ), 1.0, 6.0, ((1, 16), (2, 8), (3, 2)), jnp.float32)
    h_forward = noise(key_of[1], (3, NX, NY, NZ), 1.0, 6.0, ((1, 16), (2, 8), (3, 2)), jnp.float32)
    e_adjoint = noise(key_of[2], (3, NX, NY, NZ), 1.0, 6.0, ((1, 16), (2, 8), (3, 2)), jnp.float32)
    h_adjoint = noise(key_of[3], (3, NX, NY, NZ), 1.0, 6.0, ((1, 16), (2, 8), (3, 2)), jnp.float32)
    material = place_ends(jax.random.randint(key_of[4], (NX, NY, NZ), 0, 4), jax.random.fold_in(key_of[4], 1), 0, 3).astype(jnp.int32)
    dft_forward = noise(key_of[5], (FREQS, 2, 3, SLAB, NX, NY), 1.0, 6.0, ((3, 2), (4, 16), (5, 8)), jnp.float32)
    dft_adjoint = noise(key_of[6], (FREQS, 2, 3, SLAB, NX, NY), 1.0, 6.0, ((3, 2), (4, 16), (5, 8)), jnp.float32)
    angular_freq = jnp.clip(jnp.exp(jax.random.uniform(key_of[7], (FREQS,), jnp.float32, math.log(0.05), math.log(0.6))), 0.05, 0.6)
    layer_map = draw_layer_map(jax.random.fold_in(key_of[9], 71), 0)
    return dict(e_forward=e_forward, h_forward=h_forward, e_adjoint=e_adjoint, h_adjoint=h_adjoint, material=material, dft_forward=dft_forward, dft_adjoint=dft_adjoint, angular_freq=angular_freq, layer_map=layer_map)


PERMITTIVITIES = (1.0, 2.1, 4.0, 12.0)
COURANT = 0.5


def update_coefficient(material):
    result = jnp.zeros(material.shape, jnp.float32)
    for material_id, value_eps in enumerate(PERMITTIVITIES):
        result = result + jnp.where(material == material_id, COURANT / value_eps, 0.0).astype(jnp.float32)
    return result


def curl_forward(field_e, uppers):
    above_x, above_y, above_z = uppers
    comp_x = (above_y[..., 2, :, :, :] - field_e[..., 2, :, :, :]) - (above_z[..., 1, :, :, :] - field_e[..., 1, :, :, :])
    comp_y = (above_z[..., 0, :, :, :] - field_e[..., 0, :, :, :]) - (above_x[..., 2, :, :, :] - field_e[..., 2, :, :, :])
    comp_z = (above_x[..., 1, :, :, :] - field_e[..., 1, :, :, :]) - (above_y[..., 0, :, :, :] - field_e[..., 0, :, :, :])
    return jnp.stack([comp_x, comp_y, comp_z], axis=-4)


def curl_backward(field_h, lowers):
    below_x, below_y, below_z = lowers
    comp_x = (field_h[..., 2, :, :, :] - below_y[..., 2, :, :, :]) - (field_h[..., 1, :, :, :] - below_z[..., 1, :, :, :])
    comp_y = (field_h[..., 0, :, :, :] - below_z[..., 0, :, :, :]) - (field_h[..., 2, :, :, :] - below_x[..., 2, :, :, :])
    comp_z = (field_h[..., 1, :, :, :] - below_x[..., 1, :, :, :]) - (field_h[..., 0, :, :, :] - below_y[..., 0, :, :, :])
    return jnp.stack([comp_x, comp_y, comp_z], axis=-4)


def upper_cells(source, direction):
    if direction == 3:
        return jnp.concatenate([source[..., 1:], jnp.zeros_like(source[..., :1])], axis=3)
    return jnp.roll(source, -1, axis=direction)


def lower_cells(source, direction):
    if direction == 3:
        return jnp.concatenate([jnp.zeros_like(source[..., :1]), source[..., :-1]], axis=3)
    return jnp.roll(source, 1, axis=direction)


def advance(field_e, field_h, coefficient):
    uppers = tuple(upper_cells(field_e, direction) for direction in (1, 2, 3))
    new_h = field_h - COURANT * curl_forward(field_e, uppers)
    lowers = tuple(lower_cells(new_h, direction) for direction in (1, 2, 3))
    new_e = field_e + coefficient * curl_backward(new_h, lowers)
    return new_e, new_h


def reference(e_forward, h_forward, e_adjoint, h_adjoint, material, dft_forward, dft_adjoint, angular_freq, layer_map):
    coefficient = update_coefficient(material)
    e_fwd_new, h_fwd_new = advance(e_forward, h_forward, coefficient)
    e_adj_new, h_adj_new = advance(e_adjoint, h_adjoint, coefficient)
    slab_start = NZ // 2 - SLAB // 2
    phases = angular_freq * STEP
    cosine = jnp.cos(phases)[:, None, None, None, None]
    sine_term = jnp.sin(phases)[:, None, None, None, None]
    slab_fwd = jnp.transpose(e_fwd_new[:, :, :, slab_start:slab_start + SLAB], (0, 3, 1, 2))
    slab_adj = jnp.transpose(e_adj_new[:, :, :, slab_start:slab_start + SLAB], (0, 3, 1, 2))
    real_fwd = dft_forward[:, 0] + cosine * slab_fwd[None]
    imag_fwd = dft_forward[:, 1] - sine_term * slab_fwd[None]
    real_adj = dft_adjoint[:, 0] + cosine * slab_adj[None]
    imag_adj = dft_adjoint[:, 1] - sine_term * slab_adj[None]
    products = jnp.sum(real_fwd * real_adj - imag_fwd * imag_adj, axis=(0, 1))
    layers_onehot = (layer_map[None, :] == jnp.arange(LAYERS, dtype=jnp.int32)[:, None]).astype(jnp.float32)
    thickness = jnp.sum(layers_onehot, axis=1)
    summed = jnp.einsum("ls,sxy->lxy", layers_onehot, products, precision=lax.Precision.HIGHEST)
    gradient = summed / (3.0 * thickness)[:, None, None]
    return e_fwd_new, h_fwd_new, e_adj_new, h_adj_new, gradient
```

```python
import jax
import jax.numpy as jnp
from jax import lax
from jax.experimental import pallas as pl
from jax.experimental.pallas import tpu as pltpu
from jax.sharding import PartitionSpec as P

LAYERS = 16
STEP = 40
COURANT = 0.5
PERMITTIVITIES = (1.0, 2.1, 4.0, 12.0)
MESH = pl.DeviceIdType.MESH
F32 = jnp.float32
QUARTERS = 4


def step_kernel(
    ef, hf, ea, ha, mat, df, da, freq, lmap,
    ebuf, hbuf, grad,
    matb, dfb, dab, freqb, lmapb, ubuf, vbuf, gbuf, prod,
    ysend, zsend, xh, yh, zh, ysend2, zsend2, xh2, yh2, zh2, part_out, part_in,
    lsem, dsem, ssem, rsem,
):
    nx, ny, nz = mat.shape
    slab = df.shape[5]
    owned = LAYERS // 2
    gx, gy, gz = lax.axis_index("gx"), lax.axis_index("gy"), lax.axis_index("gz")
    sx, sy = lax.axis_size("gx"), lax.axis_size("gy")
    x_up, x_down = lax.rem(gx + 1, sx), lax.rem(gx + sx - 1, sx)
    y_up, y_down = lax.rem(gy + 1, sy), lax.rem(gy + sy - 1, sy)
    z_other = 1 - gz

    loads = [
        pltpu.make_async_copy(ef, ebuf.at[0, :, 0:nx, 0:ny, :], lsem.at[0]),
        pltpu.make_async_copy(ea, ebuf.at[1, :, 0:nx, 0:ny, :], lsem.at[1]),
        pltpu.make_async_copy(hf, hbuf.at[0, :, 1 : nx + 1, 8 : ny + 8, :], lsem.at[2]),
        pltpu.make_async_copy(ha, hbuf.at[1, :, 1 : nx + 1, 8 : ny + 8, :], lsem.at[3]),
        pltpu.make_async_copy(freq, freqb, lsem.at[4]),
        pltpu.make_async_copy(lmap, lmapb, lsem.at[5]),
        pltpu.make_async_copy(mat, matb, lsem.at[6]),
    ]
    for load in loads:
        load.start()
    rows = nx // QUARTERS
    dft_loads = []
    for q in range(QUARTERS):
        part = pl.ds(q * rows, rows)
        pair = (
            pltpu.make_async_copy(df.at[:, :, :, part], dfb.at[:, :, :, part], dsem.at[0, q]),
            pltpu.make_async_copy(da.at[:, :, :, part], dab.at[:, :, :, part], dsem.at[1, q]),
        )
        for load in pair:
            load.start()
        dft_loads.append(pair)

    barrier = pltpu.get_barrier_semaphore()
    for peer in ({"gx": x_up}, {"gx": x_down}, {"gy": y_up}, {"gy": y_down}, {"gz": z_other}):
        pl.semaphore_signal(barrier, inc=1, device_id=peer, device_id_type=MESH)

    lane = lax.broadcasted_iota(jnp.int32, (ny, nz), 1)

    def send(index, src, dst, peer):
        copy = pltpu.make_async_remote_copy(
            src_ref=src, dst_ref=dst, send_sem=ssem.at[index], recv_sem=rsem.at[index],
            device_id=peer, device_id_type=MESH,
        )
        copy.start()
        return copy

    def gather_lane(buf, x_off, y_off, from_lane):
        def body(x, acc):
            for r in range(2):
                for c in range(2):
                    k = (r * 2 + c) * nx + x
                    tile = buf[r, c, x + x_off, y_off : y_off + ny, :]
                    moved = pltpu.roll(tile, lax.rem(k - from_lane + nz, nz), 1)
                    acc = jnp.where(lane == k, moved, acc)
            return acc

        return lax.fori_loop(0, nx, body, jnp.zeros((ny, nz), F32))

    loads[0].wait()
    loads[1].wait()
    for r in range(2):
        for i, c in enumerate((0, 2)):
            ysend[r, i] = ebuf[r, c, 0:nx, 0, :]
    zsend[...] = gather_lane(ebuf, 0, 0, 0)
    pl.semaphore_wait(barrier, 5)
    first = [
        send(0, ebuf.at[:, 1:3, 0, 0:ny, :], xh, {"gx": x_down}),
        send(1, ysend, yh, {"gy": y_down}),
        send(2, zsend, zh, {"gz": z_other}),
    ]

    loads[4].wait()
    loads[5].wait()
    cosine, sine = [], []
    squares = None
    for f in range(df.shape[0]):
        phase = jnp.full((8, slab), freqb[f] * STEP, F32)
        cos_f, sin_f = jnp.cos(phase)[0:1], jnp.sin(phase)[0:1]
        cosine.append(cos_f)
        sine.append(sin_f)
        term = cos_f * cos_f - sin_f * sin_f
        squares = term if squares is None else squares + term
    layer_map = lmapb[...].reshape(1, 2 * slab)
    layer_ids = lax.broadcasted_iota(jnp.int32, (LAYERS, 2 * slab), 0)
    onehot_all = (layer_map == layer_ids).astype(F32)
    thickness = jnp.sum(onehot_all, axis=1, keepdims=True)
    low = gz == 0
    own_thickness = 3.0 * jnp.where(low, thickness[0:owned], thickness[owned:LAYERS])
    onehot = jnp.where(low, onehot_all[:, 0:slab], onehot_all[:, slab : 2 * slab])

    loads[2].wait()
    loads[3].wait()
    for copy in first:
        copy.wait()
    for r in range(2):
        for i in range(2):
            ebuf[r, 1 + i, nx, 0:ny, :] = xh[r, i]
            ebuf[r, 2 * i, 0:nx, ny, :] = yh[r, i]

    z_above = jnp.where(low, zh[...], 0.0)

    def h_plane(x, carry):
        for r in range(2):
            e0 = ebuf[r, 0, x, 0:ny, :]
            e1 = ebuf[r, 1, x, 0:ny, :]
            e2 = ebuf[r, 2, x, 0:ny, :]

            def up_z(value, c):
                k = (r * 2 + c) * nx + x
                edge = pltpu.roll(z_above, nz - 1 - k, 1)
                return jnp.where(lane == nz - 1, edge, pltpu.roll(value, nz - 1, 1))

            curl_x = (ebuf[r, 2, x, 1 : ny + 1, :] - e2) - (up_z(e1, 1) - e1)
            curl_y = (up_z(e0, 0) - e0) - (ebuf[r, 2, x + 1, 0:ny, :] - e2)
            curl_z = (ebuf[r, 1, x + 1, 0:ny, :] - e1) - (ebuf[r, 0, x, 1 : ny + 1, :] - e0)
            for c, curl in enumerate((curl_x, curl_y, curl_z)):
                hbuf[r, c, x + 1, 8 : ny + 8, :] = hbuf[r, c, x + 1, 8 : ny + 8, :] - COURANT * curl
        return carry

    lax.fori_loop(0, nx, h_plane, 0)

    for r in range(2):
        for i, c in enumerate((0, 2)):
            ysend2[r, i] = hbuf[r, c, 1 : nx + 1, ny + 7, :]
    zsend2[...] = gather_lane(hbuf, 1, 8, nz - 1)
    second = [
        send(3, hbuf.at[:, 1:3, nx, 8 : ny + 8, :], xh2, {"gx": x_up}),
        send(4, ysend2, yh2, {"gy": y_up}),
        send(5, zsend2, zh2, {"gz": z_other}),
    ]

    def dft_plane(x, carry):
        total = None
        for c in range(3):
            u = v = None
            for f in range(df.shape[0]):
                rf, mf = dfb[f, 0, c, x], dfb[f, 1, c, x]
                ra, ma = dab[f, 0, c, x], dab[f, 1, c, x]
                base = rf * ra - mf * ma
                total = base if total is None else total + base
                u_f = cosine[f] * ra + sine[f] * ma
                v_f = cosine[f] * rf + sine[f] * mf
                u = u_f if u is None else u + u_f
                v = v_f if v is None else v + v_f
            ubuf[c, x] = u
            vbuf[c, x] = v
        gbuf[x] = total
        return carry

    for q in range(QUARTERS):
        for load in dft_loads[q]:
            load.wait()
        lax.fori_loop(q * rows, (q + 1) * rows, dft_plane, 0)

    loads[6].wait()
    for copy in second:
        copy.wait()
    for r in range(2):
        for i in range(2):
            hbuf[r, 1 + i, 0, 8 : ny + 8, :] = xh2[r, i]
            hbuf[r, 2 * i, 1 : nx + 1, 7, :] = yh2[r, i]

    z_below = jnp.where(low, 0.0, zh2[...])
    shift = slab * z_other

    def e_plane(x, carry):
        m = matb[x]
        coefficient = jnp.where(
            m == 0, COURANT / PERMITTIVITIES[0],
            jnp.where(m == 1, COURANT / PERMITTIVITIES[1],
                      jnp.where(m == 2, COURANT / PERMITTIVITIES[2], COURANT / PERMITTIVITIES[3])),
        ).astype(F32)
        cells = []
        for r in range(2):
            h0 = hbuf[r, 0, x + 1, 8 : ny + 8, :]
            h1 = hbuf[r, 1, x + 1, 8 : ny + 8, :]
            h2 = hbuf[r, 2, x + 1, 8 : ny + 8, :]

            def down_z(value, c):
                k = (r * 2 + c) * nx + x
                edge = pltpu.roll(z_below, lax.rem(nz - k, nz), 1)
                return jnp.where(lane == 0, edge, pltpu.roll(value, 1, 1))

            curl_x = (h2 - hbuf[r, 2, x + 1, 7 : ny + 7, :]) - (h1 - down_z(h1, 1))
            curl_y = (h0 - down_z(h0, 0)) - (h2 - hbuf[r, 2, x, 8 : ny + 8, :])
            curl_z = (h1 - hbuf[r, 1, x, 8 : ny + 8, :]) - (h0 - hbuf[r, 0, x + 1, 7 : ny + 7, :])
            fields = []
            for c, curl in enumerate((curl_x, curl_y, curl_z)):
                new_e = ebuf[r, c, x, 0:ny, :] + coefficient * curl
                ebuf[r, c, x, 0:ny, :] = new_e
                fields.append(pltpu.roll(new_e, shift, 1)[:, 0:slab])
            cells.append(fields)
        total = gbuf[x]
        for c in range(3):
            fwd, adj = cells[0][c], cells[1][c]
            total = total + (fwd * (ubuf[c, x] + squares * adj) + adj * vbuf[c, x])
        prod[pl.ds(pl.multiple_of(x * ny, ny), ny), :] = total
        return carry

    lax.fori_loop(0, nx, e_plane, 0)

    sums = lax.dot_general(
        onehot, prod[...], (((1,), (1,)), ((), ())),
        precision=lax.Precision.HIGHEST, preferred_element_type=F32,
    )
    part_out[...] = jnp.where(low, sums[owned:LAYERS], sums[0:owned])
    last = send(6, part_out, part_in, {"gz": z_other})
    mine = jnp.where(low, sums[0:owned], sums[owned:LAYERS])
    last.wait()
    result = (mine + part_in[...]) / own_thickness
    for x in range(nx):
        grad[:, x, :] = result[:, x * ny : (x + 1) * ny]


def store_kernel(ebuf, hbuf, grad, oef, ohf, oea, oha, ograd, sem):
    nx, ny = oef.shape[1:3]
    copies = [
        pltpu.make_async_copy(ebuf.at[0, :, 0:nx, 0:ny, :], oef, sem.at[0]),
        pltpu.make_async_copy(hbuf.at[0, :, 1 : nx + 1, 8 : ny + 8, :], ohf, sem.at[1]),
        pltpu.make_async_copy(ebuf.at[1, :, 0:nx, 0:ny, :], oea, sem.at[2]),
        pltpu.make_async_copy(hbuf.at[1, :, 1 : nx + 1, 8 : ny + 8, :], oha, sem.at[3]),
        pltpu.make_async_copy(grad, ograd, sem.at[4]),
    ]
    for copy in copies:
        copy.start()
    for copy in copies:
        copy.wait()


def shards(ef, hf, ea, ha, mat, df, da, freq, lmap):
    comps, nx, ny, nz = ef.shape
    freqs, _, _, slab = df.shape[:4]
    df = jnp.transpose(df, (0, 1, 2, 4, 5, 3))
    da = jnp.transpose(da, (0, 1, 2, 4, 5, 3))
    args = [pltpu.with_memory_space_constraint(a, pltpu.HBM) for a in (ef, hf, ea, ha, mat, df, da, freq, lmap)]
    hbm = pl.BlockSpec(memory_space=pltpu.HBM)
    vmem = pl.BlockSpec(memory_space=pltpu.VMEM)
    padded = (2, comps, nx + 1, ny + 8, nz)
    owned = LAYERS // 2
    out = pl.pallas_call(
        step_kernel,
        name="yee_step",
        out_shape=(
            pltpu.VMEM(padded, F32),
            pltpu.VMEM(padded, F32),
            pltpu.VMEM((owned, nx, ny), F32),
        ),
        in_specs=[hbm] * 9,
        out_specs=[vmem] * 3,
        scratch_shapes=[
            pltpu.VMEM((nx, ny, nz), jnp.int32),
            pltpu.VMEM(df.shape, F32),
            pltpu.VMEM(da.shape, F32),
            pltpu.SMEM(freq.shape, F32),
            pltpu.VMEM(lmap.shape, jnp.int32),
            pltpu.VMEM((comps, nx, ny, slab), F32),
            pltpu.VMEM((comps, nx, ny, slab), F32),
            pltpu.VMEM((nx, ny, slab), F32),
            pltpu.VMEM((nx * ny, slab), F32),
            pltpu.VMEM((2, 2, nx, nz), F32),
            pltpu.VMEM((ny, nz), F32),
            pltpu.VMEM((2, 2, ny, nz), F32),
            pltpu.VMEM((2, 2, nx, nz), F32),
            pltpu.VMEM((ny, nz), F32),
            pltpu.VMEM((2, 2, nx, nz), F32),
            pltpu.VMEM((ny, nz), F32),
            pltpu.VMEM((2, 2, ny, nz), F32),
            pltpu.VMEM((2, 2, nx, nz), F32),
            pltpu.VMEM((ny, nz), F32),
            pltpu.VMEM((owned, nx * ny), F32),
            pltpu.VMEM((owned, nx * ny), F32),
            pltpu.SemaphoreType.DMA((7,)),
            pltpu.SemaphoreType.DMA((2, QUARTERS)),
            pltpu.SemaphoreType.DMA((7,)),
            pltpu.SemaphoreType.DMA((7,)),
        ],
        compiler_params=pltpu.CompilerParams(
            collective_id=0, has_side_effects=True, vmem_limit_bytes=24 << 20
        ),
    )(*args)
    staged = [pltpu.with_memory_space_constraint(o, pltpu.VMEM) for o in out]
    field = jax.ShapeDtypeStruct(ef.shape, F32)
    return pl.pallas_call(
        store_kernel,
        name="store_fields",
        out_shape=(field, field, field, field, jax.ShapeDtypeStruct((owned, nx, ny), F32)),
        in_specs=[vmem] * 3,
        out_specs=[hbm] * 5,
        scratch_shapes=[pltpu.SemaphoreType.DMA((5,))],
        compiler_params=pltpu.CompilerParams(vmem_limit_bytes=1 << 20),
    )(*staged)


def solution(mesh):
    field = P(None, "gx", "gy", "gz")
    dft = P(None, None, None, "gz", "gx", "gy")
    in_specs = (field, field, field, field, P("gx", "gy", "gz"), dft, dft, P(), P())
    out_specs = (field, field, field, field, P("gz", "gx", "gy"))
    return jax.shard_map(shards, mesh=mesh, in_specs=in_specs, out_specs=out_specs, check_vma=False)
```

```python
import jax
import jax.numpy as jnp
from jax import lax
from jax.experimental import pallas as pl
from jax.experimental.pallas import tpu as pltpu
from jax.sharding import PartitionSpec as P

LAYERS = 16
STEP = 40
COURANT = 0.5
PERMITTIVITIES = (1.0, 2.1, 4.0, 12.0)
MESH = pl.DeviceIdType.MESH
F32 = jnp.float32
QUARTERS = 4


def step_kernel(
    ef, hf, ea, ha, mat, df, da, freq, lmap,
    ebuf, hbuf, grad,
    matb, dfb, dab, freqb, lmapb, ubuf, vbuf, gbuf, prod,
    ye_out, xya_out, xyb_out, xz_out, yz_out, yp_out, z_out, part_out,
    xe, ye, xya, xyb, xz, yz, xp, yp, zf, part_in,
    lsem, dsem, ssem, rsem,
):
    nx, ny, nz = mat.shape
    freqs, slab = df.shape[0], df.shape[5]
    owned = LAYERS // 2
    gx, gy, gz = lax.axis_index("gx"), lax.axis_index("gy"), lax.axis_index("gz")
    sx, sy = lax.axis_size("gx"), lax.axis_size("gy")
    x_up, x_down = lax.rem(gx + 1, sx), lax.rem(gx + sx - 1, sx)
    y_up, y_down = lax.rem(gy + 1, sy), lax.rem(gy + sy - 1, sy)
    z_other = 1 - gz
    low = gz == 0
    x_cross = lax.rem(gx + sx + 2 * gz - 1, sx)
    y_cross = lax.rem(gy + sy + 2 * gz - 1, sy)

    loads = [
        pltpu.make_async_copy(ef, ebuf.at[0, :, 0:nx, 0:ny, :], lsem.at[0]),
        pltpu.make_async_copy(ea, ebuf.at[1, :, 0:nx, 0:ny, :], lsem.at[1]),
        pltpu.make_async_copy(hf, hbuf.at[0, :, 1 : nx + 1, 8 : ny + 8, :], lsem.at[2]),
        pltpu.make_async_copy(ha, hbuf.at[1, :, 1 : nx + 1, 8 : ny + 8, :], lsem.at[3]),
        pltpu.make_async_copy(freq, freqb, lsem.at[4]),
        pltpu.make_async_copy(lmap, lmapb, lsem.at[5]),
        pltpu.make_async_copy(mat, matb, lsem.at[6]),
    ]
    for load in loads:
        load.start()
    rows = nx // QUARTERS
    dft_loads = []
    for q in range(QUARTERS):
        part = pl.ds(q * rows, rows)
        pair = (
            pltpu.make_async_copy(df.at[:, :, :, part], dfb.at[:, :, :, part], dsem.at[0, q]),
            pltpu.make_async_copy(da.at[:, :, :, part], dab.at[:, :, :, part], dsem.at[1, q]),
        )
        for load in pair:
            load.start()
        dft_loads.append(pair)

    to_xe, to_xp = {"gx": x_down}, {"gx": x_up}
    to_ye, to_yp = {"gy": y_down}, {"gy": y_up}
    to_z = {"gz": z_other}
    to_xya, to_xyb = {"gx": x_up, "gy": y_down}, {"gx": x_down, "gy": y_up}
    to_xz, to_yz = {"gx": x_cross, "gz": z_other}, {"gy": y_cross, "gz": z_other}
    peers = (to_xe, to_xp, to_ye, to_yp, to_z, to_xya, to_xyb, to_xz, to_yz)
    barrier = pltpu.get_barrier_semaphore()
    for peer in peers:
        pl.semaphore_signal(barrier, inc=1, device_id=peer, device_id_type=MESH)

    lane = lax.broadcasted_iota(jnp.int32, (ny, nz), 1)
    row = lax.broadcasted_iota(jnp.int32, (ny, nz), 0)
    lane_x = lax.broadcasted_iota(jnp.int32, (nx, nz), 1)
    row_x = lax.broadcasted_iota(jnp.int32, (nx, nz), 0)

    def send(index, src, dst, peer):
        copy = pltpu.make_async_remote_copy(
            src_ref=src, dst_ref=dst, send_sem=ssem.at[index], recv_sem=rsem.at[index],
            device_id=peer, device_id_type=MESH,
        )
        copy.start()
        return copy

    def gather_lane(tile_of, from_lane):
        def body(x, acc):
            for r in range(2):
                for c in range(2):
                    k = (r * 2 + c) * nx + x
                    moved = pltpu.roll(tile_of(r, c, x), lax.rem(k - from_lane + nz, nz), 1)
                    acc = jnp.where(lane == k, moved, acc)
            return acc

        return lax.fori_loop(0, nx, body, jnp.zeros((ny, nz), F32))

    loads[0].wait()
    loads[1].wait()
    xz_tile = jnp.zeros((ny, nz), F32)
    yz_tile = jnp.zeros((nx, nz), F32)
    yz_row = jnp.zeros((1, nz), F32)
    for r in range(2):
        for i, c in enumerate((0, 2)):
            ye_out[r, i] = ebuf[r, c, 0:nx, 0, :]
        xya_out[r : r + 1, :] = ebuf[r, 0, nx - 1, 0:1, :]
        xyb_out[r : r + 1, :] = ebuf[r, 1, 0, ny - 1 : ny, :]
        k = r * 2 * nx + 2 * nx - 1
        column = jnp.where(
            low, pltpu.roll(ebuf[r, 2, 0, 0:ny, :], k + 1, 1), pltpu.roll(ebuf[r, 0, nx - 1, 0:ny, :], k, 1)
        )
        xz_tile = jnp.where(lane == k, column, xz_tile)
        column = ebuf[r, 1, 0:nx, ny - 1, :]
        yz_tile = jnp.where(lane_x == r, column if r == 0 else pltpu.roll(column, r, 1), yz_tile)
        column = jnp.broadcast_to(ye_out[r, 1][:, nz - 1 : nz], (nx, nz))
        picked = jnp.where(lane_x == r * 2 * nx + row_x, column, 0.0)
        yz_row = yz_row + jnp.sum(picked, axis=0, keepdims=True)
    xz_out[...] = xz_tile
    yz_out[0:nx, :] = yz_tile
    yz_out[nx : nx + 8, :] = jnp.broadcast_to(yz_row, (8, nz))
    pl.semaphore_wait(barrier, len(peers))
    sent_xya = send(0, xya_out, xya, to_xya)
    sent_xyb = send(1, xyb_out, xyb, to_xyb)
    sent_ye = send(2, ye_out, ye, to_ye)
    sent_xe = send(3, ebuf.at[:, 1:3, 0, 0:ny, :], xe, to_xe)
    sent_xz = send(4, xz_out, xz, to_xz)
    sent_yz = send(5, yz_out, yz, to_yz)

    zero_row = jnp.zeros((nx, nz), F32)
    for r in range(2):
        ebuf[r, 0, 0:nx, ny, :] = zero_row
        ebuf[r, 2, 0:nx, ny, :] = zero_row
    loads[2].wait()
    loads[3].wait()

    def h_plane(x, last=False):
        for r in range(2):
            e0 = ebuf[r, 0, x, 0:ny, :]
            e1 = ebuf[r, 1, x, 0:ny, :]
            e2 = ebuf[r, 2, x, 0:ny, :]

            def up_z(value):
                return jnp.where(lane == nz - 1, 0.0, pltpu.roll(value, nz - 1, 1))

            curl_x = (ebuf[r, 2, x, 1 : ny + 1, :] - e2) - (up_z(e1) - e1)
            curl_y = up_z(e0) - e0
            curl_z = ebuf[r, 0, x, 1 : ny + 1, :] - e0
            if last:
                curl_y = curl_y + e2
                curl_z = -e1 - curl_z
            else:
                curl_y = curl_y - (ebuf[r, 2, x + 1, 0:ny, :] - e2)
                curl_z = (ebuf[r, 1, x + 1, 0:ny, :] - e1) - curl_z
            for c, curl in enumerate((curl_x, curl_y, curl_z)):
                hbuf[r, c, x + 1, 8 : ny + 8, :] = hbuf[r, c, x + 1, 8 : ny + 8, :] - COURANT * curl

    h_plane(nx - 1, last=True)
    sent_xp = send(6, hbuf.at[:, 1:3, nx, 8 : ny + 8, :], xp, to_xp)

    def h_body(x, carry):
        h_plane(x)
        return carry

    lax.fori_loop(0, nx - 1, h_body, 0)
    for r in range(2):
        for i, c in enumerate((0, 2)):
            yp_out[r, i] = hbuf[r, c, 1 : nx + 1, ny + 7, :]
    sent_yp = send(7, yp_out, yp, to_yp)
    first_e = gather_lane(lambda r, c, x: ebuf[r, 1 - c, x, 0:ny, :], 0)
    last_h = gather_lane(lambda r, c, x: hbuf[r, c, x + 1, 8 : ny + 8, :], nz - 1)
    z_out[...] = jnp.where(low, last_h, first_e)
    sent_z = send(8, z_out, zf, to_z)

    loads[4].wait()
    loads[5].wait()
    cosine, sine = [], []
    squares = None
    for f in range(freqs):
        phase = jnp.full((8, nz), freqb[f] * STEP, F32)
        cos_f, sin_f = jnp.cos(phase)[0:1], jnp.sin(phase)[0:1]
        cosine.append(cos_f[:, 0:slab])
        sine.append(sin_f[:, 0:slab])
        term = cos_f * cos_f - sin_f * sin_f
        squares = term if squares is None else squares + term
    shift = (nz - slab) * z_other
    layer_map = lmapb[...].reshape(1, 2 * slab)
    layer_ids = lax.broadcasted_iota(jnp.int32, (LAYERS, 2 * slab), 0)
    onehot_all = (layer_map == layer_ids).astype(F32)
    thickness = jnp.sum(onehot_all, axis=1, keepdims=True)
    own_thickness = 3.0 * jnp.where(low, thickness[0:owned], thickness[owned:LAYERS])

    def place(value):
        rest = jnp.zeros((value.shape[0], nz - slab), F32)
        return pltpu.roll(jnp.concatenate([value, rest], axis=1), shift, 1)

    onehot = place(jnp.where(low, onehot_all[:, 0:slab], onehot_all[:, slab : 2 * slab]))

    def dft_plane(x, carry):
        total = None
        for c in range(3):
            u = v = None
            for f in range(freqs):
                rf, mf = dfb[f, 0, c, x], dfb[f, 1, c, x]
                ra, ma = dab[f, 0, c, x], dab[f, 1, c, x]
                base = rf * ra - mf * ma
                total = base if total is None else total + base
                u_f = cosine[f] * ra + sine[f] * ma
                v_f = cosine[f] * rf + sine[f] * mf
                u = u_f if u is None else u + u_f
                v = v_f if v is None else v + v_f
            ubuf[c, x] = place(u)
            vbuf[c, x] = place(v)
        gbuf[x] = place(total)
        return carry

    for q in range(QUARTERS):
        for load in dft_loads[q]:
            load.wait()
        lax.fori_loop(q * rows, (q + 1) * rows, dft_plane, 0)
    loads[6].wait()

    half_low = jnp.where(low, COURANT, 0.0)
    sent_z.wait()
    sent_xz.wait()
    sent_yz.wait()
    z_recv = zf[...]
    xz_recv = xz[...]
    z_sign = jnp.where(lax.rem(lax.div(lane, nx), 2) == 0, COURANT, -COURANT)
    z_below = z_recv + z_sign * first_e + COURANT * xz_recv
    z_below = z_below - jnp.where(row == ny - 1, COURANT * yz[nx : nx + 1, :], 0.0)
    z_below = jnp.where(low, 0.0, z_below)
    z_above = jnp.where(low, z_sign * z_recv, 0.0)

    def z_plane(x, carry):
        for r in range(2):
            for c in range(2):
                k = (r * 2 + c) * nx + x
                edge = pltpu.roll(z_above, nz - 1 - k, 1)
                value = hbuf[r, c, x + 1, 8 : ny + 8, :]
                hbuf[r, c, x + 1, 8 : ny + 8, :] = value + jnp.where(lane == nz - 1, edge, 0.0)
        return carry

    sent_xp.wait_send()

    @pl.when(low)
    def _():
        lax.fori_loop(0, nx, z_plane, 0)

    sent_ye.wait()
    sent_yp.wait()
    sent_xyb.wait()
    for r in range(2):
        h0, h2 = hbuf[r, 0, 1 : nx + 1, ny + 7, :], hbuf[r, 2, 1 : nx + 1, ny + 7, :]
        hbuf[r, 0, 1 : nx + 1, ny + 7, :] = h0 - COURANT * ye[r, 1]
        hbuf[r, 2, 1 : nx + 1, ny + 7, :] = h2 + COURANT * ye[r, 0]
        edge = pltpu.roll(yz[0:nx, :], nz - 1 - r, 1)
        edge = jnp.where(lane_x == nz - 1, half_low * edge, 0.0)
        hbuf[r, 0, 1 : nx + 1, 7, :] = yp[r, 0] - COURANT * ye_out[r, 1] + edge
        corner = jnp.where(row_x == nx - 1, COURANT * xyb[r : r + 1, :], 0.0)
        hbuf[r, 2, 1 : nx + 1, 7, :] = yp[r, 1] + COURANT * ye_out[r, 0] - corner
    sent_xe.wait()
    sent_xp.wait_recv()
    sent_xya.wait()
    for r in range(2):
        hbuf[r, 1, nx, 8 : ny + 8, :] = hbuf[r, 1, nx, 8 : ny + 8, :] + COURANT * xe[r, 1]
        hbuf[r, 2, nx, 8 : ny + 8, :] = hbuf[r, 2, nx, 8 : ny + 8, :] - COURANT * xe[r, 0]
        k = r * 2 * nx + 2 * nx - 1
        edge = jnp.where(lane == nz - 1, half_low * pltpu.roll(xz_recv, nz - 1 - k, 1), 0.0)
        hbuf[r, 1, 0, 8 : ny + 8, :] = xp[r, 0] + COURANT * ebuf[r, 2, 0, 0:ny, :] - edge
        corner = jnp.where(row == ny - 1, COURANT * xya[r : r + 1, :], 0.0)
        hbuf[r, 2, 0, 8 : ny + 8, :] = xp[r, 1] - COURANT * ebuf[r, 1, 0, 0:ny, :] + corner

    def e_plane(x, carry):
        m = matb[x]
        coefficient = jnp.where(
            m == 0, COURANT / PERMITTIVITIES[0],
            jnp.where(m == 1, COURANT / PERMITTIVITIES[1],
                      jnp.where(m == 2, COURANT / PERMITTIVITIES[2], COURANT / PERMITTIVITIES[3])),
        ).astype(F32)
        cells = []
        for r in range(2):
            h0 = hbuf[r, 0, x + 1, 8 : ny + 8, :]
            h1 = hbuf[r, 1, x + 1, 8 : ny + 8, :]
            h2 = hbuf[r, 2, x + 1, 8 : ny + 8, :]

            def down_z(value, c):
                k = (r * 2 + c) * nx + x
                edge = pltpu.roll(z_below, lax.rem(nz - k, nz), 1)
                return jnp.where(lane == 0, edge, pltpu.roll(value, 1, 1))

            curl_x = (h2 - hbuf[r, 2, x + 1, 7 : ny + 7, :]) - (h1 - down_z(h1, 1))
            curl_y = (h0 - down_z(h0, 0)) - (h2 - hbuf[r, 2, x, 8 : ny + 8, :])
            curl_z = (h1 - hbuf[r, 1, x, 8 : ny + 8, :]) - (h0 - hbuf[r, 0, x + 1, 7 : ny + 7, :])
            fields = []
            for c, curl in enumerate((curl_x, curl_y, curl_z)):
                new_e = ebuf[r, c, x, 0:ny, :] + coefficient * curl
                ebuf[r, c, x, 0:ny, :] = new_e
                fields.append(new_e)
            cells.append(fields)
        total = gbuf[x]
        for c in range(3):
            fwd, adj = cells[0][c], cells[1][c]
            total = total + (fwd * (ubuf[c, x] + squares * adj) + adj * vbuf[c, x])
        prod[pl.ds(pl.multiple_of(x * ny, ny), ny), :] = total
        return carry

    lax.fori_loop(0, nx, e_plane, 0)

    sums = lax.dot_general(
        onehot, prod[...], (((1,), (1,)), ((), ())),
        precision=lax.Precision.HIGHEST, preferred_element_type=F32,
    )
    part_out[...] = jnp.where(low, sums[owned:LAYERS], sums[0:owned])
    last = send(9, part_out, part_in, to_z)
    mine = jnp.where(low, sums[0:owned], sums[owned:LAYERS])
    last.wait()
    result = (mine + part_in[...]) / own_thickness
    for x in range(nx):
        grad[:, x, :] = result[:, x * ny : (x + 1) * ny]


def store_kernel(ebuf, hbuf, grad, oef, ohf, oea, oha, ograd, sem):
    nx, ny = oef.shape[1:3]
    copies = [
        pltpu.make_async_copy(ebuf.at[0, :, 0:nx, 0:ny, :], oef, sem.at[0]),
        pltpu.make_async_copy(hbuf.at[0, :, 1 : nx + 1, 8 : ny + 8, :], ohf, sem.at[1]),
        pltpu.make_async_copy(ebuf.at[1, :, 0:nx, 0:ny, :], oea, sem.at[2]),
        pltpu.make_async_copy(hbuf.at[1, :, 1 : nx + 1, 8 : ny + 8, :], oha, sem.at[3]),
        pltpu.make_async_copy(grad, ograd, sem.at[4]),
    ]
    for copy in copies:
        copy.start()
    for copy in copies:
        copy.wait()


def shards(ef, hf, ea, ha, mat, df, da, freq, lmap):
    comps, nx, ny, nz = ef.shape
    freqs, _, _, slab = df.shape[:4]
    df = jnp.transpose(df, (0, 1, 2, 4, 5, 3))
    da = jnp.transpose(da, (0, 1, 2, 4, 5, 3))
    args = [pltpu.with_memory_space_constraint(a, pltpu.HBM) for a in (ef, hf, ea, ha, mat, df, da, freq, lmap)]
    hbm = pl.BlockSpec(memory_space=pltpu.HBM)
    vmem = pl.BlockSpec(memory_space=pltpu.VMEM)
    padded = (2, comps, nx + 1, ny + 8, nz)
    owned = LAYERS // 2
    out = pl.pallas_call(
        step_kernel,
        name="yee_step",
        out_shape=(
            pltpu.VMEM(padded, F32),
            pltpu.VMEM(padded, F32),
            pltpu.VMEM((owned, nx, ny), F32),
        ),
        in_specs=[hbm] * 9,
        out_specs=[vmem] * 3,
        scratch_shapes=[
            pltpu.VMEM((nx, ny, nz), jnp.int32),
            pltpu.VMEM(df.shape, F32),
            pltpu.VMEM(da.shape, F32),
            pltpu.SMEM(freq.shape, F32),
            pltpu.VMEM(lmap.shape, jnp.int32),
            pltpu.VMEM((comps, nx, ny, nz), F32),
            pltpu.VMEM((comps, nx, ny, nz), F32),
            pltpu.VMEM((nx, ny, nz), F32),
            pltpu.VMEM((nx * ny, nz), F32),
            pltpu.VMEM((2, 2, nx, nz), F32),
            pltpu.VMEM((2, nz), F32),
            pltpu.VMEM((2, nz), F32),
            pltpu.VMEM((ny, nz), F32),
            pltpu.VMEM((nx + 8, nz), F32),
            pltpu.VMEM((2, 2, nx, nz), F32),
            pltpu.VMEM((ny, nz), F32),
            pltpu.VMEM((owned, nx * ny), F32),
            pltpu.VMEM((2, 2, ny, nz), F32),
            pltpu.VMEM((2, 2, nx, nz), F32),
            pltpu.VMEM((2, nz), F32),
            pltpu.VMEM((2, nz), F32),
            pltpu.VMEM((ny, nz), F32),
            pltpu.VMEM((nx + 8, nz), F32),
            pltpu.VMEM((2, 2, ny, nz), F32),
            pltpu.VMEM((2, 2, nx, nz), F32),
            pltpu.VMEM((ny, nz), F32),
            pltpu.VMEM((owned, nx * ny), F32),
            pltpu.SemaphoreType.DMA((7,)),
            pltpu.SemaphoreType.DMA((2, QUARTERS)),
            pltpu.SemaphoreType.DMA((10,)),
            pltpu.SemaphoreType.DMA((10,)),
        ],
        compiler_params=pltpu.CompilerParams(
            collective_id=0, has_side_effects=True, vmem_limit_bytes=24 << 20
        ),
    )(*args)
    staged = [pltpu.with_memory_space_constraint(o, pltpu.VMEM) for o in out]
    field = jax.ShapeDtypeStruct(ef.shape, F32)
    return pl.pallas_call(
        store_kernel,
        name="store_fields",
        out_shape=(field, field, field, field, jax.ShapeDtypeStruct((owned, nx, ny), F32)),
        in_specs=[vmem] * 3,
        out_specs=[hbm] * 5,
        scratch_shapes=[pltpu.SemaphoreType.DMA((5,))],
        compiler_params=pltpu.CompilerParams(vmem_limit_bytes=1 << 20),
    )(*staged)


def solution(mesh):
    field = P(None, "gx", "gy", "gz")
    dft = P(None, None, None, "gz", "gx", "gy")
    in_specs = (field, field, field, field, P("gx", "gy", "gz"), dft, dft, P(), P())
    out_specs = (field, field, field, field, P("gz", "gx", "gy"))
    return jax.shard_map(shards, mesh=mesh, in_specs=in_specs, out_specs=out_specs, check_vma=False)
```

```python
import jax
import jax.numpy as jnp
from jax import lax
from jax.experimental import pallas as pl
from jax.experimental.pallas import tpu as pltpu
from jax.sharding import PartitionSpec as P

LAYERS = 16
STEP = 40
COURANT = 0.5
PERMITTIVITIES = (1.0, 2.1, 4.0, 12.0)
MESH = pl.DeviceIdType.MESH
F32 = jnp.float32
QUARTERS = 4


def step_kernel(
    ef, hf, ea, ha, mat, df, da, freq, lmap,
    ebuf, hbuf, grad,
    matb, dfb, dab, freqb, lmapb, ubuf, vbuf, gbuf, prod, below,
    ye_out, xya_out, xyb_out, xz_out, yz_out, yp_out, z_out, part_out,
    xe, ye, xya, xyb, xz, yz, xp, yp, zf, part_in,
    lsem, dsem, ssem, rsem,
):
    nx, ny, nz = mat.shape
    freqs, slab = df.shape[0], df.shape[5]
    owned = LAYERS // 2
    gx, gy, gz = lax.axis_index("gx"), lax.axis_index("gy"), lax.axis_index("gz")
    sx, sy = lax.axis_size("gx"), lax.axis_size("gy")
    x_up, x_down = lax.rem(gx + 1, sx), lax.rem(gx + sx - 1, sx)
    y_up, y_down = lax.rem(gy + 1, sy), lax.rem(gy + sy - 1, sy)
    z_other = 1 - gz
    low = gz == 0
    x_cross = lax.rem(gx + sx + 2 * gz - 1, sx)
    y_cross = lax.rem(gy + sy + 2 * gz - 1, sy)

    loads = [
        pltpu.make_async_copy(ef, ebuf.at[0, :, 0:nx, 0:ny, :], lsem.at[0]),
        pltpu.make_async_copy(ea, ebuf.at[1, :, 0:nx, 0:ny, :], lsem.at[1]),
        pltpu.make_async_copy(hf, hbuf.at[0, :, 1 : nx + 1, 8 : ny + 8, :], lsem.at[2]),
        pltpu.make_async_copy(ha, hbuf.at[1, :, 1 : nx + 1, 8 : ny + 8, :], lsem.at[3]),
        pltpu.make_async_copy(freq, freqb, lsem.at[4]),
        pltpu.make_async_copy(lmap, lmapb, lsem.at[5]),
        pltpu.make_async_copy(mat, matb, lsem.at[6]),
    ]
    for load in loads:
        load.start()
    rows = nx // QUARTERS
    dft_loads = []
    for q in range(QUARTERS):
        part = pl.ds(q * rows, rows)
        pair = (
            pltpu.make_async_copy(df.at[:, :, :, part], dfb.at[:, :, :, part], dsem.at[0, q]),
            pltpu.make_async_copy(da.at[:, :, :, part], dab.at[:, :, :, part], dsem.at[1, q]),
        )
        dft_loads.append(pair)
    for pair in dft_loads[:2]:
        for load in pair:
            load.start()

    to_xe, to_xp = {"gx": x_down}, {"gx": x_up}
    to_ye, to_yp = {"gy": y_down}, {"gy": y_up}
    to_z = {"gz": z_other}
    to_xya, to_xyb = {"gx": x_up, "gy": y_down}, {"gx": x_down, "gy": y_up}
    to_xz, to_yz = {"gx": x_cross, "gz": z_other}, {"gy": y_cross, "gz": z_other}
    peers = (to_xe, to_xp, to_ye, to_yp, to_z, to_xya, to_xyb, to_xz, to_yz)
    barrier = pltpu.get_barrier_semaphore()
    for peer in peers:
        pl.semaphore_signal(barrier, inc=1, device_id=peer, device_id_type=MESH)

    lane = lax.broadcasted_iota(jnp.int32, (ny, nz), 1)
    row = lax.broadcasted_iota(jnp.int32, (ny, nz), 0)
    lane_x = lax.broadcasted_iota(jnp.int32, (nx, nz), 1)
    row_x = lax.broadcasted_iota(jnp.int32, (nx, nz), 0)

    def copy_to(index, src, dst, peer):
        return pltpu.make_async_remote_copy(
            src_ref=src, dst_ref=dst, send_sem=ssem.at[index], recv_sem=rsem.at[index],
            device_id=peer, device_id_type=MESH,
        )

    def send(index, src, dst, peer):
        copy = copy_to(index, src, dst, peer)
        copy.start()
        return copy

    def gather_lane(tile_of, from_lane):
        acc = jnp.zeros((ny, nz), F32)
        for k in range(4 * nx):
            tile = tile_of(k // (2 * nx), k // nx % 2, k % nx)
            by = (k - from_lane) % nz
            acc = jnp.where(lane == k, pltpu.roll(tile, by, 1) if by else tile, acc)
        return acc

    loads[0].wait()
    loads[1].wait()
    xz_tile = jnp.zeros((ny, nz), F32)
    yz_tile = jnp.zeros((nx, nz), F32)
    yz_row = jnp.zeros((1, nz), F32)
    for r in range(2):
        for i, c in enumerate((0, 2)):
            ye_out[r, i] = ebuf[r, c, 0:nx, 0, :]
        xya_out[r : r + 1, :] = ebuf[r, 0, nx - 1, 0:1, :]
        xyb_out[r : r + 1, :] = ebuf[r, 1, 0, ny - 1 : ny, :]
        k = r * 2 * nx + 2 * nx - 1
        column = jnp.where(
            low, pltpu.roll(ebuf[r, 2, 0, 0:ny, :], k + 1, 1), pltpu.roll(ebuf[r, 0, nx - 1, 0:ny, :], k, 1)
        )
        xz_tile = jnp.where(lane == k, column, xz_tile)
        column = ebuf[r, 1, 0:nx, ny - 1, :]
        yz_tile = jnp.where(lane_x == r, column if r == 0 else pltpu.roll(column, r, 1), yz_tile)
        column = jnp.broadcast_to(ye_out[r, 1][:, nz - 1 : nz], (nx, nz))
        picked = jnp.where(lane_x == r * 2 * nx + row_x, column, 0.0)
        yz_row = yz_row + jnp.sum(picked, axis=0, keepdims=True)
    xz_out[...] = xz_tile
    yz_out[0:nx, :] = yz_tile
    yz_out[nx : nx + 8, :] = jnp.broadcast_to(yz_row, (8, nz))
    pl.semaphore_wait(barrier, len(peers))
    sent_xya = send(0, xya_out, xya, to_xya)
    sent_xyb = send(1, xyb_out, xyb, to_xyb)
    sent_ye = send(2, ye_out, ye, to_ye)
    sent_xe = send(3, ebuf.at[:, 1:3, 0, 0:ny, :], xe, to_xe)
    sent_xz = send(4, xz_out, xz, to_xz)
    sent_yz = send(5, yz_out, yz, to_yz)
    sent_z = copy_to(8, z_out, zf, to_z)

    @pl.when(jnp.logical_not(low))
    def _():
        z_out[...] = gather_lane(lambda r, c, x: ebuf[r, 1 - c, x, 0:ny, :], 0)
        sent_z.start()

    below[...] = jnp.zeros_like(below)

    zero_row = jnp.zeros((nx, nz), F32)
    for r in range(2):
        ebuf[r, 0, 0:nx, ny, :] = zero_row
        ebuf[r, 2, 0:nx, ny, :] = zero_row
    loads[2].wait()
    loads[3].wait()

    def h_plane(x, last=False):
        for r in range(2):
            e0 = ebuf[r, 0, x, 0:ny, :]
            e1 = ebuf[r, 1, x, 0:ny, :]
            e2 = ebuf[r, 2, x, 0:ny, :]

            def up_z(value):
                return jnp.where(lane == nz - 1, 0.0, pltpu.roll(value, nz - 1, 1))

            curl_x = (ebuf[r, 2, x, 1 : ny + 1, :] - e2) - (up_z(e1) - e1)
            curl_y = up_z(e0) - e0
            curl_z = ebuf[r, 0, x, 1 : ny + 1, :] - e0
            if last:
                curl_y = curl_y + e2
                curl_z = -e1 - curl_z
            else:
                curl_y = curl_y - (ebuf[r, 2, x + 1, 0:ny, :] - e2)
                curl_z = (ebuf[r, 1, x + 1, 0:ny, :] - e1) - curl_z
            for c, curl in enumerate((curl_x, curl_y, curl_z)):
                hbuf[r, c, x + 1, 8 : ny + 8, :] = hbuf[r, c, x + 1, 8 : ny + 8, :] - COURANT * curl

    h_plane(nx - 1, last=True)
    sent_xp = send(6, hbuf.at[:, 1:3, nx, 8 : ny + 8, :], xp, to_xp)

    def h_body(x, carry):
        h_plane(x)
        return carry

    lax.fori_loop(0, nx - 1, h_body, 0)
    for r in range(2):
        for i, c in enumerate((0, 2)):
            yp_out[r, i] = hbuf[r, c, 1 : nx + 1, ny + 7, :]
    sent_yp = send(7, yp_out, yp, to_yp)

    @pl.when(low)
    def _():
        z_out[...] = gather_lane(lambda r, c, x: hbuf[r, c, x + 1, 8 : ny + 8, :], nz - 1)
        sent_z.start()

    for pair in dft_loads[2:]:
        for load in pair:
            load.start()

    loads[4].wait()
    loads[5].wait()
    cosine, sine = [], []
    squares = None
    for f in range(freqs):
        phase = jnp.full((8, nz), freqb[f] * STEP, F32)
        cos_f, sin_f = jnp.cos(phase)[0:1], jnp.sin(phase)[0:1]
        cosine.append(cos_f[:, 0:slab])
        sine.append(sin_f[:, 0:slab])
        term = cos_f * cos_f - sin_f * sin_f
        squares = term if squares is None else squares + term
    shift = (nz - slab) * z_other
    layer_map = lmapb[...].reshape(1, 2 * slab)
    layer_ids = lax.broadcasted_iota(jnp.int32, (LAYERS, 2 * slab), 0)
    onehot_all = (layer_map == layer_ids).astype(F32)
    thickness = jnp.sum(onehot_all, axis=1, keepdims=True)
    own_thickness = 3.0 * jnp.where(low, thickness[0:owned], thickness[owned:LAYERS])

    def place(value):
        rest = jnp.zeros((value.shape[0], nz - slab), F32)
        return pltpu.roll(jnp.concatenate([value, rest], axis=1), shift, 1)

    onehot = place(jnp.where(low, onehot_all[:, 0:slab], onehot_all[:, slab : 2 * slab]))

    def dft_plane(x, carry):
        total = None
        for c in range(3):
            u = v = None
            for f in range(freqs):
                rf, mf = dfb[f, 0, c, x], dfb[f, 1, c, x]
                ra, ma = dab[f, 0, c, x], dab[f, 1, c, x]
                base = rf * ra - mf * ma
                total = base if total is None else total + base
                u_f = cosine[f] * ra + sine[f] * ma
                v_f = cosine[f] * rf + sine[f] * mf
                u = u_f if u is None else u + u_f
                v = v_f if v is None else v + v_f
            ubuf[c, x] = place(u)
            vbuf[c, x] = place(v)
        gbuf[x] = place(total)
        return carry

    for q in range(QUARTERS):
        for load in dft_loads[q]:
            load.wait()
        lax.fori_loop(q * rows, (q + 1) * rows, dft_plane, 0)
    loads[6].wait()

    half_low = jnp.where(low, COURANT, 0.0)
    sent_z.wait()
    sent_xz.wait()
    sent_yz.wait()
    xz_recv = xz[...]
    z_sign = jnp.where(lax.rem(lax.div(lane, nx), 2) == 0, COURANT, -COURANT)
    planes = [(r, c, x, (r * 2 + c) * nx + x) for r in range(2) for c in range(2) for x in range(nx)]
    sent_xp.wait_send()

    @pl.when(low)
    def _():
        z_above = z_sign * zf[...]
        for r, c, x, k in planes:
            edge = jnp.where(lane == nz - 1, pltpu.roll(z_above, nz - 1 - k, 1), 0.0)
            hbuf[r, c, x + 1, 8 : ny + 8, :] = hbuf[r, c, x + 1, 8 : ny + 8, :] + edge

    @pl.when(jnp.logical_not(low))
    def _():
        z_below = zf[...] + z_sign * z_out[...] + COURANT * xz_recv
        z_below = z_below - jnp.where(row == ny - 1, COURANT * yz[nx : nx + 1, :], 0.0)
        for r, c, x, k in planes:
            below[r, c, x] = pltpu.roll(z_below, nz - k, 1) if k else z_below

    sent_ye.wait()
    sent_yp.wait()
    sent_xyb.wait()
    for r in range(2):
        h0, h2 = hbuf[r, 0, 1 : nx + 1, ny + 7, :], hbuf[r, 2, 1 : nx + 1, ny + 7, :]
        hbuf[r, 0, 1 : nx + 1, ny + 7, :] = h0 - COURANT * ye[r, 1]
        hbuf[r, 2, 1 : nx + 1, ny + 7, :] = h2 + COURANT * ye[r, 0]
        edge = pltpu.roll(yz[0:nx, :], nz - 1 - r, 1)
        edge = jnp.where(lane_x == nz - 1, half_low * edge, 0.0)
        hbuf[r, 0, 1 : nx + 1, 7, :] = yp[r, 0] - COURANT * ye_out[r, 1] + edge
        corner = jnp.where(row_x == nx - 1, COURANT * xyb[r : r + 1, :], 0.0)
        hbuf[r, 2, 1 : nx + 1, 7, :] = yp[r, 1] + COURANT * ye_out[r, 0] - corner
    sent_xe.wait()
    sent_xp.wait_recv()
    sent_xya.wait()
    for r in range(2):
        hbuf[r, 1, nx, 8 : ny + 8, :] = hbuf[r, 1, nx, 8 : ny + 8, :] + COURANT * xe[r, 1]
        hbuf[r, 2, nx, 8 : ny + 8, :] = hbuf[r, 2, nx, 8 : ny + 8, :] - COURANT * xe[r, 0]
        k = r * 2 * nx + 2 * nx - 1
        edge = jnp.where(lane == nz - 1, half_low * pltpu.roll(xz_recv, nz - 1 - k, 1), 0.0)
        hbuf[r, 1, 0, 8 : ny + 8, :] = xp[r, 0] + COURANT * ebuf[r, 2, 0, 0:ny, :] - edge
        corner = jnp.where(row == ny - 1, COURANT * xya[r : r + 1, :], 0.0)
        hbuf[r, 2, 0, 8 : ny + 8, :] = xp[r, 1] - COURANT * ebuf[r, 1, 0, 0:ny, :] + corner

    def e_plane(x, carry):
        m = matb[x]
        coefficient = jnp.where(
            m == 0, COURANT / PERMITTIVITIES[0],
            jnp.where(m == 1, COURANT / PERMITTIVITIES[1],
                      jnp.where(m == 2, COURANT / PERMITTIVITIES[2], COURANT / PERMITTIVITIES[3])),
        ).astype(F32)
        cells = []
        for r in range(2):
            h0 = hbuf[r, 0, x + 1, 8 : ny + 8, :]
            h1 = hbuf[r, 1, x + 1, 8 : ny + 8, :]
            h2 = hbuf[r, 2, x + 1, 8 : ny + 8, :]

            def down_z(value, c):
                return jnp.where(lane == 0, below[r, c, x], pltpu.roll(value, 1, 1))

            curl_x = (h2 - hbuf[r, 2, x + 1, 7 : ny + 7, :]) - (h1 - down_z(h1, 1))
            curl_y = (h0 - down_z(h0, 0)) - (h2 - hbuf[r, 2, x, 8 : ny + 8, :])
            curl_z = (h1 - hbuf[r, 1, x, 8 : ny + 8, :]) - (h0 - hbuf[r, 0, x + 1, 7 : ny + 7, :])
            fields = []
            for c, curl in enumerate((curl_x, curl_y, curl_z)):
                new_e = ebuf[r, c, x, 0:ny, :] + coefficient * curl
                ebuf[r, c, x, 0:ny, :] = new_e
                fields.append(new_e)
            cells.append(fields)
        total = gbuf[x]
        for c in range(3):
            fwd, adj = cells[0][c], cells[1][c]
            total = total + (fwd * (ubuf[c, x] + squares * adj) + adj * vbuf[c, x])
        prod[pl.ds(pl.multiple_of(x * ny, ny), ny), :] = total
        return carry

    lax.fori_loop(0, nx, e_plane, 0)

    sums = lax.dot_general(
        onehot, prod[...], (((1,), (1,)), ((), ())),
        precision=lax.Precision.HIGHEST, preferred_element_type=F32,
    )
    part_out[...] = jnp.where(low, sums[owned:LAYERS], sums[0:owned])
    last = send(9, part_out, part_in, to_z)
    mine = jnp.where(low, sums[0:owned], sums[owned:LAYERS])
    last.wait()
    result = (mine + part_in[...]) / own_thickness
    for x in range(nx):
        grad[:, x, :] = result[:, x * ny : (x + 1) * ny]


def store_kernel(ebuf, hbuf, grad, oef, ohf, oea, oha, ograd, sem):
    nx, ny = oef.shape[1:3]
    copies = [
        pltpu.make_async_copy(ebuf.at[0, :, 0:nx, 0:ny, :], oef, sem.at[0]),
        pltpu.make_async_copy(hbuf.at[0, :, 1 : nx + 1, 8 : ny + 8, :], ohf, sem.at[1]),
        pltpu.make_async_copy(ebuf.at[1, :, 0:nx, 0:ny, :], oea, sem.at[2]),
        pltpu.make_async_copy(hbuf.at[1, :, 1 : nx + 1, 8 : ny + 8, :], oha, sem.at[3]),
        pltpu.make_async_copy(grad, ograd, sem.at[4]),
    ]
    for copy in copies:
        copy.start()
    for copy in copies:
        copy.wait()


def shards(ef, hf, ea, ha, mat, df, da, freq, lmap):
    comps, nx, ny, nz = ef.shape
    freqs, _, _, slab = df.shape[:4]
    df = jnp.transpose(df, (0, 1, 2, 4, 5, 3))
    da = jnp.transpose(da, (0, 1, 2, 4, 5, 3))
    args = [pltpu.with_memory_space_constraint(a, pltpu.HBM) for a in (ef, hf, ea, ha, mat, df, da, freq, lmap)]
    hbm = pl.BlockSpec(memory_space=pltpu.HBM)
    vmem = pl.BlockSpec(memory_space=pltpu.VMEM)
    padded = (2, comps, nx + 1, ny + 8, nz)
    owned = LAYERS // 2
    out = pl.pallas_call(
        step_kernel,
        name="yee_step",
        out_shape=(
            pltpu.VMEM(padded, F32),
            pltpu.VMEM(padded, F32),
            pltpu.VMEM((owned, nx, ny), F32),
        ),
        in_specs=[hbm] * 9,
        out_specs=[vmem] * 3,
        scratch_shapes=[
            pltpu.VMEM((nx, ny, nz), jnp.int32),
            pltpu.VMEM(df.shape, F32),
            pltpu.VMEM(da.shape, F32),
            pltpu.SMEM(freq.shape, F32),
            pltpu.VMEM(lmap.shape, jnp.int32),
            pltpu.VMEM((comps, nx, ny, nz), F32),
            pltpu.VMEM((comps, nx, ny, nz), F32),
            pltpu.VMEM((nx, ny, nz), F32),
            pltpu.VMEM((nx * ny, nz), F32),
            pltpu.VMEM((2, 2, nx, ny, nz), F32),
            pltpu.VMEM((2, 2, nx, nz), F32),
            pltpu.VMEM((2, nz), F32),
            pltpu.VMEM((2, nz), F32),
            pltpu.VMEM((ny, nz), F32),
            pltpu.VMEM((nx + 8, nz), F32),
            pltpu.VMEM((2, 2, nx, nz), F32),
            pltpu.VMEM((ny, nz), F32),
            pltpu.VMEM((owned, nx * ny), F32),
            pltpu.VMEM((2, 2, ny, nz), F32),
            pltpu.VMEM((2, 2, nx, nz), F32),
            pltpu.VMEM((2, nz), F32),
            pltpu.VMEM((2, nz), F32),
            pltpu.VMEM((ny, nz), F32),
            pltpu.VMEM((nx + 8, nz), F32),
            pltpu.VMEM((2, 2, ny, nz), F32),
            pltpu.VMEM((2, 2, nx, nz), F32),
            pltpu.VMEM((ny, nz), F32),
            pltpu.VMEM((owned, nx * ny), F32),
            pltpu.SemaphoreType.DMA((7,)),
            pltpu.SemaphoreType.DMA((2, QUARTERS)),
            pltpu.SemaphoreType.DMA((10,)),
            pltpu.SemaphoreType.DMA((10,)),
        ],
        compiler_params=pltpu.CompilerParams(
            collective_id=0, has_side_effects=True, vmem_limit_bytes=24 << 20
        ),
    )(*args)
    staged = [pltpu.with_memory_space_constraint(o, pltpu.VMEM) for o in out]
    field = jax.ShapeDtypeStruct(ef.shape, F32)
    return pl.pallas_call(
        store_kernel,
        name="store_fields",
        out_shape=(field, field, field, field, jax.ShapeDtypeStruct((owned, nx, ny), F32)),
        in_specs=[vmem] * 3,
        out_specs=[hbm] * 5,
        scratch_shapes=[pltpu.SemaphoreType.DMA((5,))],
        compiler_params=pltpu.CompilerParams(vmem_limit_bytes=1 << 20),
    )(*staged)


def solution(mesh):
    field = P(None, "gx", "gy", "gz")
    dft = P(None, None, None, "gz", "gx", "gy")
    in_specs = (field, field, field, field, P("gx", "gy", "gz"), dft, dft, P(), P())
    out_specs = (field, field, field, field, P("gz", "gx", "gy"))
    return jax.shard_map(shards, mesh=mesh, in_specs=in_specs, out_specs=out_specs, check_vma=False)
```

```python
import jax
import jax.numpy as jnp
from jax import lax
from jax.experimental import pallas as pl
from jax.experimental.pallas import tpu as pltpu
from jax.sharding import PartitionSpec as P

LAYERS = 16
STEP = 40
COURANT = 0.5
PERMITTIVITIES = (1.0, 2.1, 4.0, 12.0)
MESH = pl.DeviceIdType.MESH
F32 = jnp.float32
QUARTERS = 4


def step_kernel(
    ef, hf, ea, ha, mat, df, da, freq, lmap,
    ebuf, hbuf, grad,
    matb, dfb, dab, freqb, lmapb, ubuf, vbuf, gbuf, prod, below,
    ye_out, xya_out, xyb_out, xz_out, yz_out, yp_out, z_out, part_out,
    xe, ye, xya, xyb, xz, yz, xp, yp, zf, part_in,
    lsem, dsem, ssem, rsem,
):
    nx, ny, nz = mat.shape
    freqs, slab = df.shape[0], df.shape[5]
    owned = LAYERS // 2
    gx, gy, gz = lax.axis_index("gx"), lax.axis_index("gy"), lax.axis_index("gz")
    sx, sy = lax.axis_size("gx"), lax.axis_size("gy")
    x_up, x_down = lax.rem(gx + 1, sx), lax.rem(gx + sx - 1, sx)
    y_up, y_down = lax.rem(gy + 1, sy), lax.rem(gy + sy - 1, sy)
    z_other = 1 - gz
    low = gz == 0
    x_cross = lax.rem(gx + sx + 2 * gz - 1, sx)
    y_cross = lax.rem(gy + sy + 2 * gz - 1, sy)

    to_xe, to_xp = {"gx": x_down}, {"gx": x_up}
    to_ye, to_yp = {"gy": y_down}, {"gy": y_up}
    to_z = {"gz": z_other}
    to_xya, to_xyb = {"gx": x_up, "gy": y_down}, {"gx": x_down, "gy": y_up}
    to_xz, to_yz = {"gx": x_cross, "gz": z_other}, {"gy": y_cross, "gz": z_other}
    peers = (to_xe, to_xp, to_ye, to_yp, to_z, to_xya, to_xyb, to_xz, to_yz)
    barrier = pltpu.get_barrier_semaphore()
    for peer in peers:
        pl.semaphore_signal(barrier, inc=1, device_id=peer, device_id_type=MESH)

    loads = [
        pltpu.make_async_copy(ef, ebuf.at[0, :, 0:nx, 0:ny, :], lsem.at[0]),
        pltpu.make_async_copy(ea, ebuf.at[1, :, 0:nx, 0:ny, :], lsem.at[1]),
        pltpu.make_async_copy(hf, hbuf.at[0, :, 1 : nx + 1, 8 : ny + 8, :], lsem.at[2]),
        pltpu.make_async_copy(ha, hbuf.at[1, :, 1 : nx + 1, 8 : ny + 8, :], lsem.at[3]),
        pltpu.make_async_copy(freq, freqb, lsem.at[4]),
        pltpu.make_async_copy(lmap, lmapb, lsem.at[5]),
        pltpu.make_async_copy(mat, matb, lsem.at[6]),
    ]
    for load in loads:
        load.start()
    rows = nx // QUARTERS
    dft_loads = []
    for q in range(QUARTERS):
        part = pl.ds(q * rows, rows)
        pair = (
            pltpu.make_async_copy(df.at[:, :, :, part], dfb.at[:, :, :, part], dsem.at[0, q]),
            pltpu.make_async_copy(da.at[:, :, :, part], dab.at[:, :, :, part], dsem.at[1, q]),
        )
        dft_loads.append(pair)
    for pair in dft_loads[:2]:
        for load in pair:
            load.start()

    lane = lax.broadcasted_iota(jnp.int32, (ny, nz), 1)
    row = lax.broadcasted_iota(jnp.int32, (ny, nz), 0)
    lane_x = lax.broadcasted_iota(jnp.int32, (nx, nz), 1)
    row_x = lax.broadcasted_iota(jnp.int32, (nx, nz), 0)

    def copy_to(index, src, dst, peer):
        return pltpu.make_async_remote_copy(
            src_ref=src, dst_ref=dst, send_sem=ssem.at[index], recv_sem=rsem.at[index],
            device_id=peer, device_id_type=MESH,
        )

    def send(index, src, dst, peer):
        copy = copy_to(index, src, dst, peer)
        copy.start()
        return copy

    def gather_lane(tile_of, from_lane):
        acc = jnp.zeros((ny, nz), F32)
        for k in range(4 * nx):
            tile = tile_of(k // (2 * nx), k // nx % 2, k % nx)
            by = (k - from_lane) % nz
            acc = jnp.where(lane == k, pltpu.roll(tile, by, 1) if by else tile, acc)
        return acc

    loads[0].wait()
    loads[1].wait()
    xz_tile = jnp.zeros((ny, nz), F32)
    yz_tile = jnp.zeros((nx, nz), F32)
    yz_row = jnp.zeros((1, nz), F32)
    for r in range(2):
        for i, c in enumerate((0, 2)):
            ye_out[r, i] = ebuf[r, c, 0:nx, 0, :]
        xya_out[r : r + 1, :] = ebuf[r, 0, nx - 1, 0:1, :]
        xyb_out[r : r + 1, :] = ebuf[r, 1, 0, ny - 1 : ny, :]
        k = r * 2 * nx + 2 * nx - 1
        column = jnp.where(
            low, pltpu.roll(ebuf[r, 2, 0, 0:ny, :], k + 1, 1), pltpu.roll(ebuf[r, 0, nx - 1, 0:ny, :], k, 1)
        )
        xz_tile = jnp.where(lane == k, column, xz_tile)
        column = ebuf[r, 1, 0:nx, ny - 1, :]
        yz_tile = jnp.where(lane_x == r, column if r == 0 else pltpu.roll(column, r, 1), yz_tile)
        column = jnp.broadcast_to(ye_out[r, 1][:, nz - 1 : nz], (nx, nz))
        picked = jnp.where(lane_x == r * 2 * nx + row_x, column, 0.0)
        yz_row = yz_row + jnp.sum(picked, axis=0, keepdims=True)
    xz_out[...] = xz_tile
    yz_out[0:nx, :] = yz_tile
    yz_out[nx : nx + 8, :] = jnp.broadcast_to(yz_row, (8, nz))

    @pl.when(jnp.logical_not(low))
    def _():
        z_out[...] = gather_lane(lambda r, c, x: ebuf[r, 1 - c, x, 0:ny, :], 0)


    zero_row = jnp.zeros((nx, nz), F32)
    for r in range(2):
        ebuf[r, 0, 0:nx, ny, :] = zero_row
        ebuf[r, 2, 0:nx, ny, :] = zero_row
    loads[2].wait()
    loads[3].wait()

    def h_plane(x, last=False):
        for r in range(2):
            e0 = ebuf[r, 0, x, 0:ny, :]
            e1 = ebuf[r, 1, x, 0:ny, :]
            e2 = ebuf[r, 2, x, 0:ny, :]

            def up_z(value):
                return jnp.where(lane == nz - 1, 0.0, pltpu.roll(value, nz - 1, 1))

            curl_x = (ebuf[r, 2, x, 1 : ny + 1, :] - e2) - (up_z(e1) - e1)
            curl_y = up_z(e0) - e0
            curl_z = ebuf[r, 0, x, 1 : ny + 1, :] - e0
            if last:
                curl_y = curl_y + e2
                curl_z = -e1 - curl_z
            else:
                curl_y = curl_y - (ebuf[r, 2, x + 1, 0:ny, :] - e2)
                curl_z = (ebuf[r, 1, x + 1, 0:ny, :] - e1) - curl_z
            for c, curl in enumerate((curl_x, curl_y, curl_z)):
                hbuf[r, c, x + 1, 8 : ny + 8, :] = hbuf[r, c, x + 1, 8 : ny + 8, :] - COURANT * curl

    h_plane(nx - 1, last=True)

    def h_body(x, carry):
        h_plane(x)
        return carry

    lax.fori_loop(0, nx - 1, h_body, 0, unroll=3)
    for r in range(2):
        for i, c in enumerate((0, 2)):
            yp_out[r, i] = hbuf[r, c, 1 : nx + 1, ny + 7, :]

    @pl.when(low)
    def _():
        z_out[...] = gather_lane(lambda r, c, x: hbuf[r, c, x + 1, 8 : ny + 8, :], nz - 1)

    pl.semaphore_wait(barrier, len(peers))
    sent_xe = send(3, ebuf.at[:, 1:3, 0, 0:ny, :], xe, to_xe)
    sent_xz = send(4, xz_out, xz, to_xz)
    sent_xya = send(0, xya_out, xya, to_xya)
    sent_xyb = send(1, xyb_out, xyb, to_xyb)
    sent_z = send(8, z_out, zf, to_z)
    sent_yp = send(7, yp_out, yp, to_yp)
    sent_ye = send(2, ye_out, ye, to_ye)
    sent_xp = send(6, hbuf.at[:, 1:3, nx, 8 : ny + 8, :], xp, to_xp)
    sent_yz = send(5, yz_out, yz, to_yz)
    below[...] = jnp.zeros_like(below)
    for pair in dft_loads[2:]:
        for load in pair:
            load.start()

    loads[4].wait()
    loads[5].wait()
    cosine, sine = [], []
    squares = None
    for f in range(freqs):
        phase = jnp.full((8, nz), freqb[f] * STEP, F32)
        cos_f, sin_f = jnp.cos(phase)[0:1], jnp.sin(phase)[0:1]
        cosine.append(cos_f[:, 0:slab])
        sine.append(sin_f[:, 0:slab])
        term = cos_f * cos_f - sin_f * sin_f
        squares = term if squares is None else squares + term
    shift = (nz - slab) * z_other
    layer_map = lmapb[...].reshape(1, 2 * slab)
    layer_ids = lax.broadcasted_iota(jnp.int32, (LAYERS, 2 * slab), 0)
    onehot_all = (layer_map == layer_ids).astype(F32)
    thickness = jnp.sum(onehot_all, axis=1, keepdims=True)
    own_thickness = 3.0 * jnp.where(low, thickness[0:owned], thickness[owned:LAYERS])

    def place(value):
        rest = jnp.zeros((value.shape[0], nz - slab), F32)
        return pltpu.roll(jnp.concatenate([value, rest], axis=1), shift, 1)

    onehot = place(jnp.where(low, onehot_all[:, 0:slab], onehot_all[:, slab : 2 * slab]))

    def dft_plane(x, carry):
        total = None
        for c in range(3):
            u = v = None
            for f in range(freqs):
                rf, mf = dfb[f, 0, c, x], dfb[f, 1, c, x]
                ra, ma = dab[f, 0, c, x], dab[f, 1, c, x]
                base = rf * ra - mf * ma
                total = base if total is None else total + base
                u_f = cosine[f] * ra + sine[f] * ma
                v_f = cosine[f] * rf + sine[f] * mf
                u = u_f if u is None else u + u_f
                v = v_f if v is None else v + v_f
            ubuf[c, x] = place(u)
            vbuf[c, x] = place(v)
        gbuf[x] = place(total)
        return carry

    for q in range(QUARTERS):
        for load in dft_loads[q]:
            load.wait()
        lax.fori_loop(q * rows, (q + 1) * rows, dft_plane, 0, unroll=2)
    loads[6].wait()

    half_low = jnp.where(low, COURANT, 0.0)
    sent_z.wait()
    sent_xz.wait()
    sent_yz.wait()
    xz_recv = xz[...]
    z_sign = jnp.where(lax.rem(lax.div(lane, nx), 2) == 0, COURANT, -COURANT)
    planes = [(r, c, x, (r * 2 + c) * nx + x) for r in range(2) for c in range(2) for x in range(nx)]
    sent_xp.wait_send()

    @pl.when(low)
    def _():
        z_above = z_sign * zf[...]
        for r, c, x, k in planes:
            edge = jnp.where(lane == nz - 1, pltpu.roll(z_above, nz - 1 - k, 1), 0.0)
            hbuf[r, c, x + 1, 8 : ny + 8, :] = hbuf[r, c, x + 1, 8 : ny + 8, :] + edge

    @pl.when(jnp.logical_not(low))
    def _():
        z_below = zf[...] + z_sign * z_out[...] + COURANT * xz_recv
        z_below = z_below - jnp.where(row == ny - 1, COURANT * yz[nx : nx + 1, :], 0.0)
        for r, c, x, k in planes:
            below[r, c, x] = pltpu.roll(z_below, nz - k, 1) if k else z_below

    sent_ye.wait()
    sent_yp.wait()
    sent_xyb.wait()
    for r in range(2):
        h0, h2 = hbuf[r, 0, 1 : nx + 1, ny + 7, :], hbuf[r, 2, 1 : nx + 1, ny + 7, :]
        hbuf[r, 0, 1 : nx + 1, ny + 7, :] = h0 - COURANT * ye[r, 1]
        hbuf[r, 2, 1 : nx + 1, ny + 7, :] = h2 + COURANT * ye[r, 0]
        edge = pltpu.roll(yz[0:nx, :], nz - 1 - r, 1)
        edge = jnp.where(lane_x == nz - 1, half_low * edge, 0.0)
        hbuf[r, 0, 1 : nx + 1, 7, :] = yp[r, 0] - COURANT * ye_out[r, 1] + edge
        corner = jnp.where(row_x == nx - 1, COURANT * xyb[r : r + 1, :], 0.0)
        hbuf[r, 2, 1 : nx + 1, 7, :] = yp[r, 1] + COURANT * ye_out[r, 0] - corner
    sent_xe.wait()
    sent_xp.wait_recv()
    sent_xya.wait()
    for r in range(2):
        hbuf[r, 1, nx, 8 : ny + 8, :] = hbuf[r, 1, nx, 8 : ny + 8, :] + COURANT * xe[r, 1]
        hbuf[r, 2, nx, 8 : ny + 8, :] = hbuf[r, 2, nx, 8 : ny + 8, :] - COURANT * xe[r, 0]
        k = r * 2 * nx + 2 * nx - 1
        edge = jnp.where(lane == nz - 1, half_low * pltpu.roll(xz_recv, nz - 1 - k, 1), 0.0)
        hbuf[r, 1, 0, 8 : ny + 8, :] = xp[r, 0] + COURANT * ebuf[r, 2, 0, 0:ny, :] - edge
        corner = jnp.where(row == ny - 1, COURANT * xya[r : r + 1, :], 0.0)
        hbuf[r, 2, 0, 8 : ny + 8, :] = xp[r, 1] - COURANT * ebuf[r, 1, 0, 0:ny, :] + corner

    def e_plane(x, carry):
        m = matb[x]
        coefficient = jnp.where(
            m == 0, COURANT / PERMITTIVITIES[0],
            jnp.where(m == 1, COURANT / PERMITTIVITIES[1],
                      jnp.where(m == 2, COURANT / PERMITTIVITIES[2], COURANT / PERMITTIVITIES[3])),
        ).astype(F32)
        cells = []
        for r in range(2):
            h0 = hbuf[r, 0, x + 1, 8 : ny + 8, :]
            h1 = hbuf[r, 1, x + 1, 8 : ny + 8, :]
            h2 = hbuf[r, 2, x + 1, 8 : ny + 8, :]

            def down_z(value, c):
                return jnp.where(lane == 0, below[r, c, x], pltpu.roll(value, 1, 1))

            curl_x = (h2 - hbuf[r, 2, x + 1, 7 : ny + 7, :]) - (h1 - down_z(h1, 1))
            curl_y = (h0 - down_z(h0, 0)) - (h2 - hbuf[r, 2, x, 8 : ny + 8, :])
            curl_z = (h1 - hbuf[r, 1, x, 8 : ny + 8, :]) - (h0 - hbuf[r, 0, x + 1, 7 : ny + 7, :])
            fields = []
            for c, curl in enumerate((curl_x, curl_y, curl_z)):
                new_e = ebuf[r, c, x, 0:ny, :] + coefficient * curl
                ebuf[r, c, x, 0:ny, :] = new_e
                fields.append(new_e)
            cells.append(fields)
        total = gbuf[x]
        for c in range(3):
            fwd, adj = cells[0][c], cells[1][c]
            total = total + (fwd * (ubuf[c, x] + squares * adj) + adj * vbuf[c, x])
        prod[pl.ds(pl.multiple_of(x * ny, ny), ny), :] = total
        return carry

    lax.fori_loop(0, nx, e_plane, 0, unroll=2)

    sums = lax.dot_general(
        onehot, prod[...], (((1,), (1,)), ((), ())),
        precision=lax.Precision.HIGHEST, preferred_element_type=F32,
    )
    part_out[...] = jnp.where(low, sums[owned:LAYERS], sums[0:owned])
    last = send(9, part_out, part_in, to_z)
    mine = jnp.where(low, sums[0:owned], sums[owned:LAYERS])
    last.wait()
    result = (mine + part_in[...]) / own_thickness
    for x in range(nx):
        grad[:, x, :] = result[:, x * ny : (x + 1) * ny]


def store_kernel(ebuf, hbuf, grad, oef, ohf, oea, oha, ograd, sem):
    nx, ny = oef.shape[1:3]
    copies = [
        pltpu.make_async_copy(ebuf.at[0, :, 0:nx, 0:ny, :], oef, sem.at[0]),
        pltpu.make_async_copy(hbuf.at[0, :, 1 : nx + 1, 8 : ny + 8, :], ohf, sem.at[1]),
        pltpu.make_async_copy(ebuf.at[1, :, 0:nx, 0:ny, :], oea, sem.at[2]),
        pltpu.make_async_copy(hbuf.at[1, :, 1 : nx + 1, 8 : ny + 8, :], oha, sem.at[3]),
        pltpu.make_async_copy(grad, ograd, sem.at[4]),
    ]
    for copy in copies:
        copy.start()
    for copy in copies:
        copy.wait()


def shards(ef, hf, ea, ha, mat, df, da, freq, lmap):
    comps, nx, ny, nz = ef.shape
    freqs, _, _, slab = df.shape[:4]
    df = jnp.transpose(df, (0, 1, 2, 4, 5, 3))
    da = jnp.transpose(da, (0, 1, 2, 4, 5, 3))
    args = [pltpu.with_memory_space_constraint(a, pltpu.HBM) for a in (ef, hf, ea, ha, mat, df, da, freq, lmap)]
    hbm = pl.BlockSpec(memory_space=pltpu.HBM)
    vmem = pl.BlockSpec(memory_space=pltpu.VMEM)
    padded = (2, comps, nx + 1, ny + 8, nz)
    owned = LAYERS // 2
    out = pl.pallas_call(
        step_kernel,
        name="yee_step",
        out_shape=(
            pltpu.VMEM(padded, F32),
            pltpu.VMEM(padded, F32),
            pltpu.VMEM((owned, nx, ny), F32),
        ),
        in_specs=[hbm] * 9,
        out_specs=[vmem] * 3,
        scratch_shapes=[
            pltpu.VMEM((nx, ny, nz), jnp.int32),
            pltpu.VMEM(df.shape, F32),
            pltpu.VMEM(da.shape, F32),
            pltpu.SMEM(freq.shape, F32),
            pltpu.VMEM(lmap.shape, jnp.int32),
            pltpu.VMEM((comps, nx, ny, nz), F32),
            pltpu.VMEM((comps, nx, ny, nz), F32),
            pltpu.VMEM((nx, ny, nz), F32),
            pltpu.VMEM((nx * ny, nz), F32),
            pltpu.VMEM((2, 2, nx, ny, nz), F32),
            pltpu.VMEM((2, 2, nx, nz), F32),
            pltpu.VMEM((2, nz), F32),
            pltpu.VMEM((2, nz), F32),
            pltpu.VMEM((ny, nz), F32),
            pltpu.VMEM((nx + 8, nz), F32),
            pltpu.VMEM((2, 2, nx, nz), F32),
            pltpu.VMEM((ny, nz), F32),
            pltpu.VMEM((owned, nx * ny), F32),
            pltpu.VMEM((2, 2, ny, nz), F32),
            pltpu.VMEM((2, 2, nx, nz), F32),
            pltpu.VMEM((2, nz), F32),
            pltpu.VMEM((2, nz), F32),
            pltpu.VMEM((ny, nz), F32),
            pltpu.VMEM((nx + 8, nz), F32),
            pltpu.VMEM((2, 2, ny, nz), F32),
            pltpu.VMEM((2, 2, nx, nz), F32),
            pltpu.VMEM((ny, nz), F32),
            pltpu.VMEM((owned, nx * ny), F32),
            pltpu.SemaphoreType.DMA((7,)),
            pltpu.SemaphoreType.DMA((2, QUARTERS)),
            pltpu.SemaphoreType.DMA((10,)),
            pltpu.SemaphoreType.DMA((10,)),
        ],
        compiler_params=pltpu.CompilerParams(
            collective_id=0, has_side_effects=True, vmem_limit_bytes=24 << 20
        ),
    )(*args)
    staged = [pltpu.with_memory_space_constraint(o, pltpu.VMEM) for o in out]
    field = jax.ShapeDtypeStruct(ef.shape, F32)
    return pl.pallas_call(
        store_kernel,
        name="store_fields",
        out_shape=(field, field, field, field, jax.ShapeDtypeStruct((owned, nx, ny), F32)),
        in_specs=[vmem] * 3,
        out_specs=[hbm] * 5,
        scratch_shapes=[pltpu.SemaphoreType.DMA((5,))],
        compiler_params=pltpu.CompilerParams(vmem_limit_bytes=1 << 20),
    )(*staged)


def solution(mesh):
    field = P(None, "gx", "gy", "gz")
    dft = P(None, None, None, "gz", "gx", "gy")
    in_specs = (field, field, field, field, P("gx", "gy", "gz"), dft, dft, P(), P())
    out_specs = (field, field, field, field, P("gz", "gx", "gy"))
    return jax.shard_map(shards, mesh=mesh, in_specs=in_specs, out_specs=out_specs, check_vma=False)
```

```python
import jax
import jax.numpy as jnp
from jax import lax
from jax.experimental import pallas as pl
from jax.experimental.pallas import tpu as pltpu
from jax.sharding import PartitionSpec as P

LAYERS = 16
STEP = 40
COURANT = 0.5
PERMITTIVITIES = (1.0, 2.1, 4.0, 12.0)
MESH = pl.DeviceIdType.MESH
F32 = jnp.float32
QUARTERS = 4


def step_kernel(
    ef, hf, ea, ha, mat, df, da, freq, lmap,
    ebuf, hbuf, grad,
    matb, dfb, dab, freqb, lmapb, ubuf, vbuf, gbuf, prod, below,
    ye_out, xya_out, xyb_out, xz_out, yz_out, yp_out, z_out, part_out,
    xe, ye, xya, xyb, xz, yz, xp, yp, zf, part_in,
    fsem, lsem, dsem, ssem, rsem,
):
    nx, ny, nz = mat.shape
    freqs, slab = df.shape[0], df.shape[5]
    owned = LAYERS // 2
    gx, gy, gz = lax.axis_index("gx"), lax.axis_index("gy"), lax.axis_index("gz")
    sx, sy = lax.axis_size("gx"), lax.axis_size("gy")
    x_up, x_down = lax.rem(gx + 1, sx), lax.rem(gx + sx - 1, sx)
    y_up, y_down = lax.rem(gy + 1, sy), lax.rem(gy + sy - 1, sy)
    z_other = 1 - gz
    low = gz == 0
    x_cross = lax.rem(gx + sx + 2 * gz - 1, sx)
    y_cross = lax.rem(gy + sy + 2 * gz - 1, sy)

    to_xe, to_xp = {"gx": x_down}, {"gx": x_up}
    to_ye, to_yp = {"gy": y_down}, {"gy": y_up}
    to_z = {"gz": z_other}
    to_xya, to_xyb = {"gx": x_up, "gy": y_down}, {"gx": x_down, "gy": y_up}
    to_xz, to_yz = {"gx": x_cross, "gz": z_other}, {"gy": y_cross, "gz": z_other}
    peers = (to_xe, to_xp, to_ye, to_yp, to_z, to_xya, to_xyb, to_xz, to_yz)
    barrier = pltpu.get_barrier_semaphore()
    for peer in peers:
        pl.semaphore_signal(barrier, inc=1, device_id=peer, device_id_type=MESH)

    rows = nx // QUARTERS
    field_loads = []
    for q in reversed(range(QUARTERS)):
        part, inner = pl.ds(q * rows, rows), pl.ds(q * rows + 1, rows)
        group = [
            pltpu.make_async_copy(ef.at[:, part], ebuf.at[0, :, part, 0:ny, :], fsem.at[0, q]),
            pltpu.make_async_copy(ea.at[:, part], ebuf.at[1, :, part, 0:ny, :], fsem.at[1, q]),
            pltpu.make_async_copy(hf.at[:, part], hbuf.at[0, :, inner, 8 : ny + 8, :], fsem.at[2, q]),
            pltpu.make_async_copy(ha.at[:, part], hbuf.at[1, :, inner, 8 : ny + 8, :], fsem.at[3, q]),
        ]
        for load in group:
            load.start()
        field_loads.append((q, group))
    loads = [
        pltpu.make_async_copy(freq, freqb, lsem.at[0]),
        pltpu.make_async_copy(lmap, lmapb, lsem.at[1]),
        pltpu.make_async_copy(mat, matb, lsem.at[2]),
    ]
    for load in loads:
        load.start()
    dft_loads = []
    for q in range(QUARTERS):
        part = pl.ds(q * rows, rows)
        pair = (
            pltpu.make_async_copy(df.at[:, :, :, part], dfb.at[:, :, :, part], dsem.at[0, q]),
            pltpu.make_async_copy(da.at[:, :, :, part], dab.at[:, :, :, part], dsem.at[1, q]),
        )
        dft_loads.append(pair)
    for pair in dft_loads[:2]:
        for load in pair:
            load.start()

    lane = lax.broadcasted_iota(jnp.int32, (ny, nz), 1)
    row = lax.broadcasted_iota(jnp.int32, (ny, nz), 0)
    lane_x = lax.broadcasted_iota(jnp.int32, (nx, nz), 1)
    row_x = lax.broadcasted_iota(jnp.int32, (nx, nz), 0)

    def copy_to(index, src, dst, peer):
        return pltpu.make_async_remote_copy(
            src_ref=src, dst_ref=dst, send_sem=ssem.at[index], recv_sem=rsem.at[index],
            device_id=peer, device_id_type=MESH,
        )

    def send(index, src, dst, peer):
        copy = copy_to(index, src, dst, peer)
        copy.start()
        return copy

    def gather_lane(tile_of, from_lane, first):
        acc = z_out[...]
        for k in range(4 * nx):
            if first <= k % nx < first + rows:
                tile = tile_of(k // (2 * nx), k // nx % 2, k % nx)
                by = (k - from_lane) % nz
                acc = jnp.where(lane == k, pltpu.roll(tile, by, 1) if by else tile, acc)
        z_out[...] = acc

    zero_row = jnp.zeros((nx, nz), F32)
    for r in range(2):
        ebuf[r, 0, 0:nx, ny, :] = zero_row
        ebuf[r, 2, 0:nx, ny, :] = zero_row
    z_out[...] = jnp.zeros_like(z_out)

    def h_plane(x, last=False):
        for r in range(2):
            e0 = ebuf[r, 0, x, 0:ny, :]
            e1 = ebuf[r, 1, x, 0:ny, :]
            e2 = ebuf[r, 2, x, 0:ny, :]

            def up_z(value):
                return jnp.where(lane == nz - 1, 0.0, pltpu.roll(value, nz - 1, 1))

            curl_x = (ebuf[r, 2, x, 1 : ny + 1, :] - e2) - (up_z(e1) - e1)
            curl_y = up_z(e0) - e0
            curl_z = ebuf[r, 0, x, 1 : ny + 1, :] - e0
            if last:
                curl_y = curl_y + e2
                curl_z = -e1 - curl_z
            else:
                curl_y = curl_y - (ebuf[r, 2, x + 1, 0:ny, :] - e2)
                curl_z = (ebuf[r, 1, x + 1, 0:ny, :] - e1) - curl_z
            for c, curl in enumerate((curl_x, curl_y, curl_z)):
                hbuf[r, c, x + 1, 8 : ny + 8, :] = hbuf[r, c, x + 1, 8 : ny + 8, :] - COURANT * curl

    def h_body(x, carry):
        h_plane(x)
        return carry

    for q, group in field_loads:
        for load in group:
            load.wait()
        if q == QUARTERS - 1:
            h_plane(nx - 1, last=True)
        lax.fori_loop(q * rows, min((q + 1) * rows, nx - 1), h_body, 0, unroll=True)

        @pl.when(low)
        def _():
            gather_lane(lambda r, c, x: hbuf[r, c, x + 1, 8 : ny + 8, :], nz - 1, q * rows)

        @pl.when(jnp.logical_not(low))
        def _():
            gather_lane(lambda r, c, x: ebuf[r, 1 - c, x, 0:ny, :], 0, q * rows)

    for r in range(2):
        for i, c in enumerate((0, 2)):
            yp_out[r, i] = hbuf[r, c, 1 : nx + 1, ny + 7, :]

    xz_tile = jnp.zeros((ny, nz), F32)
    yz_tile = jnp.zeros((nx, nz), F32)
    yz_row = jnp.zeros((1, nz), F32)
    for r in range(2):
        for i, c in enumerate((0, 2)):
            ye_out[r, i] = ebuf[r, c, 0:nx, 0, :]
        xya_out[r : r + 1, :] = ebuf[r, 0, nx - 1, 0:1, :]
        xyb_out[r : r + 1, :] = ebuf[r, 1, 0, ny - 1 : ny, :]
        k = r * 2 * nx + 2 * nx - 1
        column = jnp.where(
            low, pltpu.roll(ebuf[r, 2, 0, 0:ny, :], k + 1, 1), pltpu.roll(ebuf[r, 0, nx - 1, 0:ny, :], k, 1)
        )
        xz_tile = jnp.where(lane == k, column, xz_tile)
        column = ebuf[r, 1, 0:nx, ny - 1, :]
        yz_tile = jnp.where(lane_x == r, column if r == 0 else pltpu.roll(column, r, 1), yz_tile)
        column = jnp.broadcast_to(ye_out[r, 1][:, nz - 1 : nz], (nx, nz))
        picked = jnp.where(lane_x == r * 2 * nx + row_x, column, 0.0)
        yz_row = yz_row + jnp.sum(picked, axis=0, keepdims=True)
    xz_out[...] = xz_tile
    yz_out[0:nx, :] = yz_tile
    yz_out[nx : nx + 8, :] = jnp.broadcast_to(yz_row, (8, nz))

    pl.semaphore_wait(barrier, len(peers))
    sent_xya = send(0, xya_out, xya, to_xya)
    sent_xyb = send(1, xyb_out, xyb, to_xyb)
    sent_xz = send(4, xz_out, xz, to_xz)
    sent_yz = send(5, yz_out, yz, to_yz)
    sent_z = send(8, z_out, zf, to_z)
    sent_yp = send(7, yp_out, yp, to_yp)
    sent_ye = send(2, ye_out, ye, to_ye)
    sent_xp = send(6, hbuf.at[:, 1:3, nx, 8 : ny + 8, :], xp, to_xp)
    sent_xe = send(3, ebuf.at[:, 1:3, 0, 0:ny, :], xe, to_xe)
    for pair in dft_loads[2:]:
        for load in pair:
            load.start()
    below[...] = jnp.zeros_like(below)
    loads[0].wait()
    loads[1].wait()
    cosine, sine = [], []
    squares = None
    for f in range(freqs):
        phase = jnp.full((8, nz), freqb[f] * STEP, F32)
        cos_f, sin_f = jnp.cos(phase)[0:1], jnp.sin(phase)[0:1]
        cosine.append(cos_f[:, 0:slab])
        sine.append(sin_f[:, 0:slab])
        term = cos_f * cos_f - sin_f * sin_f
        squares = term if squares is None else squares + term
    shift = (nz - slab) * z_other
    layer_map = lmapb[...].reshape(1, 2 * slab)
    layer_ids = lax.broadcasted_iota(jnp.int32, (LAYERS, 2 * slab), 0)
    onehot_all = (layer_map == layer_ids).astype(F32)
    thickness = jnp.sum(onehot_all, axis=1, keepdims=True)
    own_thickness = 3.0 * jnp.where(low, thickness[0:owned], thickness[owned:LAYERS])

    def place(value):
        rest = jnp.zeros((value.shape[0], nz - slab), F32)
        return pltpu.roll(jnp.concatenate([value, rest], axis=1), shift, 1)

    onehot = place(jnp.where(low, onehot_all[:, 0:slab], onehot_all[:, slab : 2 * slab]))

    def dft_plane(x, carry):
        total = None
        for c in range(3):
            u = v = None
            for f in range(freqs):
                rf, mf = dfb[f, 0, c, x], dfb[f, 1, c, x]
                ra, ma = dab[f, 0, c, x], dab[f, 1, c, x]
                base = rf * ra - mf * ma
                total = base if total is None else total + base
                u_f = cosine[f] * ra + sine[f] * ma
                v_f = cosine[f] * rf + sine[f] * mf
                u = u_f if u is None else u + u_f
                v = v_f if v is None else v + v_f
            ubuf[c, x] = place(u)
            vbuf[c, x] = place(v)
        gbuf[x] = place(total)
        return carry

    for q in range(QUARTERS):
        for load in dft_loads[q]:
            load.wait()
        lax.fori_loop(q * rows, (q + 1) * rows, dft_plane, 0, unroll=2)
    loads[2].wait()

    half_low = jnp.where(low, COURANT, 0.0)
    half_high = COURANT - half_low
    sent_z.wait()
    sent_yz.wait()
    z_sign = jnp.where(lax.rem(lax.div(lane, nx), 2) == 0, COURANT, -COURANT)
    places = [(r, c, x, (r * 2 + c) * nx + x) for r in range(2) for c in range(2) for x in range(nx)]
    last_x = nx - 1

    def add_above(r, c, x, k):
        edge = jnp.where(lane == nz - 1, pltpu.roll(z_sign * zf[...], nz - 1 - k, 1), 0.0)
        hbuf[r, c, x + 1, 8 : ny + 8, :] = hbuf[r, c, x + 1, 8 : ny + 8, :] + edge

    @pl.when(low)
    def _():
        for r, c, x, k in places:
            if x < last_x:
                add_above(r, c, x, k)

    @pl.when(jnp.logical_not(low))
    def _():
        z_below = zf[...] + z_sign * z_out[...]
        z_below = z_below - jnp.where(row == ny - 1, COURANT * yz[nx : nx + 1, :], 0.0)
        for r, c, x, k in places:
            below[r, c, x] = pltpu.roll(z_below, nz - k, 1) if k else z_below

    sent_ye.wait()
    sent_yp.wait()
    for r in range(2):
        h0, h2 = hbuf[r, 0, 1:nx, ny + 7, :], hbuf[r, 2, 1:nx, ny + 7, :]
        hbuf[r, 0, 1:nx, ny + 7, :] = h0 - COURANT * ye[r, 1, 0:last_x]
        hbuf[r, 2, 1:nx, ny + 7, :] = h2 + COURANT * ye[r, 0, 0:last_x]
        edge = pltpu.roll(yz[0:nx, :], nz - 1 - r, 1)
        edge = jnp.where(lane_x == nz - 1, half_low * edge, 0.0)
        hbuf[r, 0, 1 : nx + 1, 7, :] = yp[r, 0] - COURANT * ye_out[r, 1] + edge
        hbuf[r, 2, 1 : nx + 1, 7, :] = yp[r, 1] + COURANT * ye_out[r, 0]

    def e_plane(x, carry):
        m = matb[x]
        coefficient = jnp.where(
            m == 0, COURANT / PERMITTIVITIES[0],
            jnp.where(m == 1, COURANT / PERMITTIVITIES[1],
                      jnp.where(m == 2, COURANT / PERMITTIVITIES[2], COURANT / PERMITTIVITIES[3])),
        ).astype(F32)
        cells = []
        for r in range(2):
            h0 = hbuf[r, 0, x + 1, 8 : ny + 8, :]
            h1 = hbuf[r, 1, x + 1, 8 : ny + 8, :]
            h2 = hbuf[r, 2, x + 1, 8 : ny + 8, :]

            def down_z(value, c):
                return jnp.where(lane == 0, below[r, c, x], pltpu.roll(value, 1, 1))

            curl_x = (h2 - hbuf[r, 2, x + 1, 7 : ny + 7, :]) - (h1 - down_z(h1, 1))
            curl_y = (h0 - down_z(h0, 0)) - (h2 - hbuf[r, 2, x, 8 : ny + 8, :])
            curl_z = (h1 - hbuf[r, 1, x, 8 : ny + 8, :]) - (h0 - hbuf[r, 0, x + 1, 7 : ny + 7, :])
            fields = []
            for c, curl in enumerate((curl_x, curl_y, curl_z)):
                new_e = ebuf[r, c, x, 0:ny, :] + coefficient * curl
                ebuf[r, c, x, 0:ny, :] = new_e
                fields.append(new_e)
            cells.append(fields)
        total = gbuf[x]
        for c in range(3):
            fwd, adj = cells[0][c], cells[1][c]
            total = total + (fwd * (ubuf[c, x] + squares * adj) + adj * vbuf[c, x])
        prod[pl.ds(pl.multiple_of(x * ny, ny) if not isinstance(x, int) else x * ny, ny), :] = total
        return carry

    lax.fori_loop(1, last_x, e_plane, 0, unroll=2)

    sent_xe.wait()
    sent_xp.wait()
    sent_xz.wait()
    sent_xya.wait()
    sent_xyb.wait()

    @pl.when(low)
    def _():
        for r, c, x, k in places:
            if x == last_x:
                add_above(r, c, x, k)

    for r in range(2):
        row_0, row_2 = hbuf[r, 0, nx, ny + 7 : ny + 8, :], hbuf[r, 2, nx, ny + 7 : ny + 8, :]
        hbuf[r, 0, nx, ny + 7 : ny + 8, :] = row_0 - COURANT * ye[r, 1, last_x:nx, :]
        hbuf[r, 2, nx, ny + 7 : ny + 8, :] = row_2 + COURANT * ye[r, 0, last_x:nx, :]
        hbuf[r, 2, nx, 7:8, :] = hbuf[r, 2, nx, 7:8, :] - COURANT * xyb[r : r + 1, :]
        hbuf[r, 1, nx, 8 : ny + 8, :] = hbuf[r, 1, nx, 8 : ny + 8, :] + COURANT * xe[r, 1]
        hbuf[r, 2, nx, 8 : ny + 8, :] = hbuf[r, 2, nx, 8 : ny + 8, :] - COURANT * xe[r, 0]
        k = r * 2 * nx + 2 * nx - 1
        column = pltpu.roll(xz[...], nz - k, 1)
        below[r, 1, last_x] = below[r, 1, last_x] + half_high * column
        edge = jnp.where(lane == nz - 1, half_low * pltpu.roll(column, nz - 1, 1), 0.0)
        hbuf[r, 1, 0, 8 : ny + 8, :] = xp[r, 0] + COURANT * ebuf[r, 2, 0, 0:ny, :] - edge
        corner = jnp.where(row == ny - 1, COURANT * xya[r : r + 1, :], 0.0)
        hbuf[r, 2, 0, 8 : ny + 8, :] = xp[r, 1] - COURANT * ebuf[r, 1, 0, 0:ny, :] + corner

    e_plane(0, 0)
    e_plane(last_x, 0)

    sums = lax.dot_general(
        onehot, prod[...], (((1,), (1,)), ((), ())),
        precision=lax.Precision.HIGHEST, preferred_element_type=F32,
    )
    part_out[...] = jnp.where(low, sums[owned:LAYERS], sums[0:owned])
    last = send(9, part_out, part_in, to_z)
    mine = jnp.where(low, sums[0:owned], sums[owned:LAYERS])
    last.wait()
    result = (mine + part_in[...]) / own_thickness
    for x in range(nx):
        grad[:, x, :] = result[:, x * ny : (x + 1) * ny]


def store_kernel(ebuf, hbuf, grad, oef, ohf, oea, oha, ograd, sem):
    nx, ny = oef.shape[1:3]
    copies = [
        pltpu.make_async_copy(ebuf.at[0, :, 0:nx, 0:ny, :], oef, sem.at[0]),
        pltpu.make_async_copy(hbuf.at[0, :, 1 : nx + 1, 8 : ny + 8, :], ohf, sem.at[1]),
        pltpu.make_async_copy(ebuf.at[1, :, 0:nx, 0:ny, :], oea, sem.at[2]),
        pltpu.make_async_copy(hbuf.at[1, :, 1 : nx + 1, 8 : ny + 8, :], oha, sem.at[3]),
        pltpu.make_async_copy(grad, ograd, sem.at[4]),
    ]
    for copy in copies:
        copy.start()
    for copy in copies:
        copy.wait()


def shards(ef, hf, ea, ha, mat, df, da, freq, lmap):
    comps, nx, ny, nz = ef.shape
    freqs, _, _, slab = df.shape[:4]
    df = jnp.transpose(df, (0, 1, 2, 4, 5, 3))
    da = jnp.transpose(da, (0, 1, 2, 4, 5, 3))
    args = [pltpu.with_memory_space_constraint(a, pltpu.HBM) for a in (ef, hf, ea, ha, mat, df, da, freq, lmap)]
    hbm = pl.BlockSpec(memory_space=pltpu.HBM)
    vmem = pl.BlockSpec(memory_space=pltpu.VMEM)
    padded = (2, comps, nx + 1, ny + 8, nz)
    owned = LAYERS // 2
    out = pl.pallas_call(
        step_kernel,
        name="yee_step",
        out_shape=(
            pltpu.VMEM(padded, F32),
            pltpu.VMEM(padded, F32),
            pltpu.VMEM((owned, nx, ny), F32),
        ),
        in_specs=[hbm] * 9,
        out_specs=[vmem] * 3,
        scratch_shapes=[
            pltpu.VMEM((nx, ny, nz), jnp.int32),
            pltpu.VMEM(df.shape, F32),
            pltpu.VMEM(da.shape, F32),
            pltpu.SMEM(freq.shape, F32),
            pltpu.VMEM(lmap.shape, jnp.int32),
            pltpu.VMEM((comps, nx, ny, nz), F32),
            pltpu.VMEM((comps, nx, ny, nz), F32),
            pltpu.VMEM((nx, ny, nz), F32),
            pltpu.VMEM((nx * ny, nz), F32),
            pltpu.VMEM((2, 2, nx, ny, nz), F32),
            pltpu.VMEM((2, 2, nx, nz), F32),
            pltpu.VMEM((2, nz), F32),
            pltpu.VMEM((2, nz), F32),
            pltpu.VMEM((ny, nz), F32),
            pltpu.VMEM((nx + 8, nz), F32),
            pltpu.VMEM((2, 2, nx, nz), F32),
            pltpu.VMEM((ny, nz), F32),
            pltpu.VMEM((owned, nx * ny), F32),
            pltpu.VMEM((2, 2, ny, nz), F32),
            pltpu.VMEM((2, 2, nx, nz), F32),
            pltpu.VMEM((2, nz), F32),
            pltpu.VMEM((2, nz), F32),
            pltpu.VMEM((ny, nz), F32),
            pltpu.VMEM((nx + 8, nz), F32),
            pltpu.VMEM((2, 2, ny, nz), F32),
            pltpu.VMEM((2, 2, nx, nz), F32),
            pltpu.VMEM((ny, nz), F32),
            pltpu.VMEM((owned, nx * ny), F32),
            pltpu.SemaphoreType.DMA((4, QUARTERS)),
            pltpu.SemaphoreType.DMA((3,)),
            pltpu.SemaphoreType.DMA((2, QUARTERS)),
            pltpu.SemaphoreType.DMA((10,)),
            pltpu.SemaphoreType.DMA((10,)),
        ],
        compiler_params=pltpu.CompilerParams(
            collective_id=0, has_side_effects=True, vmem_limit_bytes=24 << 20
        ),
    )(*args)
    staged = [pltpu.with_memory_space_constraint(o, pltpu.VMEM) for o in out]
    field = jax.ShapeDtypeStruct(ef.shape, F32)
    return pl.pallas_call(
        store_kernel,
        name="store_fields",
        out_shape=(field, field, field, field, jax.ShapeDtypeStruct((owned, nx, ny), F32)),
        in_specs=[vmem] * 3,
        out_specs=[hbm] * 5,
        scratch_shapes=[pltpu.SemaphoreType.DMA((5,))],
        compiler_params=pltpu.CompilerParams(vmem_limit_bytes=1 << 20),
    )(*staged)


def solution(mesh):
    field = P(None, "gx", "gy", "gz")
    dft = P(None, None, None, "gz", "gx", "gy")
    in_specs = (field, field, field, field, P("gx", "gy", "gz"), dft, dft, P(), P())
    out_specs = (field, field, field, field, P("gz", "gx", "gy"))
    return jax.shard_map(shards, mesh=mesh, in_specs=in_specs, out_specs=out_specs, check_vma=False)
```

```python
import jax
import jax.numpy as jnp
from jax import lax
from jax.experimental import pallas as pl
from jax.experimental.pallas import tpu as pltpu
from jax.sharding import PartitionSpec as P

LAYERS = 16
STEP = 40
COURANT = 0.5
PERMITTIVITIES = (1.0, 2.1, 4.0, 12.0)
MESH = pl.DeviceIdType.MESH
F32 = jnp.float32
QUARTERS = 4


def step_kernel(
    ef, hf, ea, ha, mat, df, da, freq, lmap,
    ebuf, hbuf, grad,
    matb, dfb, dab, freqb, lmapb, ubuf, vbuf, gbuf, prod, below,
    ye_out, xya_out, xyb_out, xz_out, yz_out, yp_out, z_out, part_out,
    xe, ye, xya, xyb, xz, yz, xp, yp, zf, part_in,
    fsem, lsem, dsem, ssem, rsem,
):
    nx, ny, nz = mat.shape
    freqs, slab = df.shape[0], df.shape[5]
    owned = LAYERS // 2
    gx, gy, gz = lax.axis_index("gx"), lax.axis_index("gy"), lax.axis_index("gz")
    sx, sy = lax.axis_size("gx"), lax.axis_size("gy")
    x_up, x_down = lax.rem(gx + 1, sx), lax.rem(gx + sx - 1, sx)
    y_up, y_down = lax.rem(gy + 1, sy), lax.rem(gy + sy - 1, sy)
    z_other = 1 - gz
    low = gz == 0
    x_cross = lax.rem(gx + sx + 2 * gz - 1, sx)
    y_cross = lax.rem(gy + sy + 2 * gz - 1, sy)

    to_xe, to_xp = {"gx": x_down}, {"gx": x_up}
    to_ye, to_yp = {"gy": y_down}, {"gy": y_up}
    to_z = {"gz": z_other}
    to_xya, to_xyb = {"gx": x_up, "gy": y_down}, {"gx": x_down, "gy": y_up}
    to_xz, to_yz = {"gx": x_cross, "gz": z_other}, {"gy": y_cross, "gz": z_other}
    peers = (to_xe, to_xp, to_ye, to_yp, to_z, to_xya, to_xyb, to_xz, to_yz)
    barrier = pltpu.get_barrier_semaphore()
    for peer in peers:
        pl.semaphore_signal(barrier, inc=1, device_id=peer, device_id_type=MESH)

    rows = nx // QUARTERS
    field_loads = []
    for q in reversed(range(QUARTERS)):
        part, inner = pl.ds(q * rows, rows), pl.ds(q * rows + 1, rows)
        group = [
            pltpu.make_async_copy(ef.at[:, part], ebuf.at[0, :, part, 0:ny, :], fsem.at[0, q]),
            pltpu.make_async_copy(ea.at[:, part], ebuf.at[1, :, part, 0:ny, :], fsem.at[1, q]),
            pltpu.make_async_copy(hf.at[:, part], hbuf.at[0, :, inner, 8 : ny + 8, :], fsem.at[2, q]),
            pltpu.make_async_copy(ha.at[:, part], hbuf.at[1, :, inner, 8 : ny + 8, :], fsem.at[3, q]),
        ]
        for load in group:
            load.start()
        field_loads.append((q, group))
    loads = [
        pltpu.make_async_copy(freq, freqb, lsem.at[0]),
        pltpu.make_async_copy(lmap, lmapb, lsem.at[1]),
        pltpu.make_async_copy(mat, matb, lsem.at[2]),
    ]
    for load in loads:
        load.start()
    dft_loads = []
    for q in range(QUARTERS):
        part = pl.ds(q * rows, rows)
        pair = (
            pltpu.make_async_copy(df.at[:, :, :, part], dfb.at[:, :, :, part], dsem.at[0, q]),
            pltpu.make_async_copy(da.at[:, :, :, part], dab.at[:, :, :, part], dsem.at[1, q]),
        )
        dft_loads.append(pair)
    for pair in dft_loads[:2]:
        for load in pair:
            load.start()

    lane = lax.broadcasted_iota(jnp.int32, (ny, nz), 1)
    row = lax.broadcasted_iota(jnp.int32, (ny, nz), 0)
    lane_x = lax.broadcasted_iota(jnp.int32, (nx, nz), 1)
    row_x = lax.broadcasted_iota(jnp.int32, (nx, nz), 0)

    def copy_to(index, src, dst, peer):
        return pltpu.make_async_remote_copy(
            src_ref=src, dst_ref=dst, send_sem=ssem.at[index], recv_sem=rsem.at[index],
            device_id=peer, device_id_type=MESH,
        )

    def send(index, src, dst, peer):
        copy = copy_to(index, src, dst, peer)
        copy.start()
        return copy

    def gather_lane(tile_of, from_lane, first):
        acc = z_out[...]
        for k in range(4 * nx):
            if first <= k % nx < first + rows:
                tile = tile_of(k // (2 * nx), k // nx % 2, k % nx)
                by = (k - from_lane) % nz
                acc = jnp.where(lane == k, pltpu.roll(tile, by, 1) if by else tile, acc)
        z_out[...] = acc

    zero_row = jnp.zeros((nx, nz), F32)
    for r in range(2):
        ebuf[r, 0, 0:nx, ny, :] = zero_row
        ebuf[r, 2, 0:nx, ny, :] = zero_row
    z_out[...] = jnp.zeros_like(z_out)

    def h_plane(x, last=False):
        for r in range(2):
            e0 = ebuf[r, 0, x, 0:ny, :]
            e1 = ebuf[r, 1, x, 0:ny, :]
            e2 = ebuf[r, 2, x, 0:ny, :]

            def up_z(value):
                return jnp.where(lane == nz - 1, 0.0, pltpu.roll(value, nz - 1, 1))

            curl_x = (ebuf[r, 2, x, 1 : ny + 1, :] - e2) - (up_z(e1) - e1)
            curl_y = up_z(e0) - e0
            curl_z = ebuf[r, 0, x, 1 : ny + 1, :] - e0
            if last:
                curl_y = curl_y + e2
                curl_z = -e1 - curl_z
            else:
                curl_y = curl_y - (ebuf[r, 2, x + 1, 0:ny, :] - e2)
                curl_z = (ebuf[r, 1, x + 1, 0:ny, :] - e1) - curl_z
            for c, curl in enumerate((curl_x, curl_y, curl_z)):
                hbuf[r, c, x + 1, 8 : ny + 8, :] = hbuf[r, c, x + 1, 8 : ny + 8, :] - COURANT * curl

    def h_body(x, carry):
        h_plane(x)
        return carry

    for q, group in field_loads:
        for load in group:
            load.wait()
        if q == QUARTERS - 1:
            h_plane(nx - 1, last=True)
        lax.fori_loop(q * rows, min((q + 1) * rows, nx - 1), h_body, 0, unroll=True)

        @pl.when(low)
        def _():
            gather_lane(lambda r, c, x: hbuf[r, c, x + 1, 8 : ny + 8, :], nz - 1, q * rows)

        @pl.when(jnp.logical_not(low))
        def _():
            gather_lane(lambda r, c, x: ebuf[r, 1 - c, x, 0:ny, :], 0, q * rows)

    for r in range(2):
        for i, c in enumerate((0, 2)):
            yp_out[r, i] = hbuf[r, c, 1 : nx + 1, ny + 7, :]

    xz_tile = jnp.zeros((ny, nz), F32)
    yz_tile = jnp.zeros((nx, nz), F32)
    yz_row = jnp.zeros((1, nz), F32)
    for r in range(2):
        for i, c in enumerate((0, 2)):
            ye_out[r, i] = ebuf[r, c, 0:nx, 0, :]
        xya_out[r : r + 1, :] = ebuf[r, 0, nx - 1, 0:1, :]
        xyb_out[r : r + 1, :] = ebuf[r, 1, 0, ny - 1 : ny, :]
        k = r * 2 * nx + 2 * nx - 1
        column = jnp.where(
            low, pltpu.roll(ebuf[r, 2, 0, 0:ny, :], k + 1, 1), pltpu.roll(ebuf[r, 0, nx - 1, 0:ny, :], k, 1)
        )
        xz_tile = jnp.where(lane == k, column, xz_tile)
        column = ebuf[r, 1, 0:nx, ny - 1, :]
        yz_tile = jnp.where(lane_x == r, column if r == 0 else pltpu.roll(column, r, 1), yz_tile)
        column = jnp.broadcast_to(ye_out[r, 1][:, nz - 1 : nz], (nx, nz))
        picked = jnp.where(lane_x == r * 2 * nx + row_x, column, 0.0)
        yz_row = yz_row + jnp.sum(picked, axis=0, keepdims=True)
    xz_out[...] = xz_tile
    yz_out[0:nx, :] = yz_tile
    yz_out[nx : nx + 8, :] = jnp.broadcast_to(yz_row, (8, nz))

    pl.semaphore_wait(barrier, len(peers))
    sent_xya = send(0, xya_out, xya, to_xya)
    sent_xyb = send(1, xyb_out, xyb, to_xyb)
    sent_xz = send(4, xz_out, xz, to_xz)
    sent_yz = send(5, yz_out, yz, to_yz)
    sent_z = send(8, z_out, zf, to_z)
    sent_yp = send(7, yp_out, yp, to_yp)
    sent_ye = send(2, ye_out, ye, to_ye)
    sent_xp = send(6, hbuf.at[:, 1:3, nx, 8 : ny + 8, :], xp, to_xp)
    sent_xe = send(3, ebuf.at[:, 1:3, 0, 0:ny, :], xe, to_xe)
    for pair in dft_loads[2:]:
        for load in pair:
            load.start()
    below[...] = jnp.zeros_like(below)
    loads[0].wait()
    loads[1].wait()
    cosine, sine = [], []
    squares = None
    for f in range(freqs):
        phase = jnp.full((8, nz), freqb[f] * STEP, F32)
        cos_f, sin_f = jnp.cos(phase)[0:1], jnp.sin(phase)[0:1]
        cosine.append(cos_f[:, 0:slab])
        sine.append(sin_f[:, 0:slab])
        term = cos_f * cos_f - sin_f * sin_f
        squares = term if squares is None else squares + term
    shift = (nz - slab) * z_other
    layer_map = lmapb[...].reshape(1, 2 * slab)
    layer_ids = lax.broadcasted_iota(jnp.int32, (LAYERS, 2 * slab), 0)
    onehot_all = (layer_map == layer_ids).astype(F32)
    thickness = jnp.sum(onehot_all, axis=1, keepdims=True)
    own_thickness = 3.0 * jnp.where(low, thickness[0:owned], thickness[owned:LAYERS])

    def place(value):
        rest = jnp.zeros((value.shape[0], nz - slab), F32)
        return pltpu.roll(jnp.concatenate([value, rest], axis=1), shift, 1)

    onehot = place(jnp.where(low, onehot_all[:, 0:slab], onehot_all[:, slab : 2 * slab]))

    def dft_plane(x, carry):
        total = None
        for c in range(3):
            u = v = None
            for f in range(freqs):
                rf, mf = dfb[f, 0, c, x], dfb[f, 1, c, x]
                ra, ma = dab[f, 0, c, x], dab[f, 1, c, x]
                base = rf * ra - mf * ma
                total = base if total is None else total + base
                u_f = cosine[f] * ra + sine[f] * ma
                v_f = cosine[f] * rf + sine[f] * mf
                u = u_f if u is None else u + u_f
                v = v_f if v is None else v + v_f
            ubuf[c, x] = place(u)
            vbuf[c, x] = place(v)
        gbuf[x] = place(total)
        return carry

    for q in range(QUARTERS):
        for load in dft_loads[q]:
            load.wait()
        lax.fori_loop(q * rows, (q + 1) * rows, dft_plane, 0, unroll=2)
    loads[2].wait()

    half_low = jnp.where(low, COURANT, 0.0)
    half_high = COURANT - half_low
    sent_z.wait()
    z_sign = jnp.where(lax.rem(lax.div(lane, nx), 2) == 0, COURANT, -COURANT)
    places = [(r, c, x, (r * 2 + c) * nx + x) for r in range(2) for c in range(2) for x in range(nx)]
    last_x = nx - 1

    def add_above(r, c, x, k):
        edge = jnp.where(lane == nz - 1, pltpu.roll(z_sign * zf[...], nz - 1 - k, 1), 0.0)
        hbuf[r, c, x + 1, 8 : ny + 8, :] = hbuf[r, c, x + 1, 8 : ny + 8, :] + edge

    @pl.when(low)
    def _():
        for r, c, x, k in places:
            if x < last_x:
                add_above(r, c, x, k)

    @pl.when(jnp.logical_not(low))
    def _():
        z_below = zf[...] + z_sign * z_out[...]
        for r, c, x, k in places:
            below[r, c, x] = pltpu.roll(z_below, nz - k, 1) if k else z_below

    def e_rows(x, y0, n):
        own, ahead = pl.ds(y0 + 8, n), pl.ds(y0 + 7, n)
        cell = pl.ds(y0, n)
        first_lane = lane[0:n] == 0
        m = matb[x, cell]
        coefficient = jnp.where(
            m == 0, COURANT / PERMITTIVITIES[0],
            jnp.where(m == 1, COURANT / PERMITTIVITIES[1],
                      jnp.where(m == 2, COURANT / PERMITTIVITIES[2], COURANT / PERMITTIVITIES[3])),
        ).astype(F32)
        cells = []
        for r in range(2):
            h0 = hbuf[r, 0, x + 1, own, :]
            h1 = hbuf[r, 1, x + 1, own, :]
            h2 = hbuf[r, 2, x + 1, own, :]

            def down_z(value, c):
                return jnp.where(first_lane, below[r, c, x, cell], pltpu.roll(value, 1, 1))

            curl_x = (h2 - hbuf[r, 2, x + 1, ahead, :]) - (h1 - down_z(h1, 1))
            curl_y = (h0 - down_z(h0, 0)) - (h2 - hbuf[r, 2, x, own, :])
            curl_z = (h1 - hbuf[r, 1, x, own, :]) - (h0 - hbuf[r, 0, x + 1, ahead, :])
            fields = []
            for c, curl in enumerate((curl_x, curl_y, curl_z)):
                new_e = ebuf[r, c, x, cell, :] + coefficient * curl
                ebuf[r, c, x, cell, :] = new_e
                fields.append(new_e)
            cells.append(fields)
        total = gbuf[x, cell]
        for c in range(3):
            fwd, adj = cells[0][c], cells[1][c]
            total = total + (fwd * (ubuf[c, x, cell] + squares * adj) + adj * vbuf[c, x, cell])
        start = x * ny + y0
        prod[pl.ds(start if isinstance(x, int) else pl.multiple_of(start, 8), n), :] = total

    half = ny // 2

    def middle_rows(x, carry):
        e_rows(x, ny // 4, half)
        return carry

    def outer_rows(x, carry):
        e_rows(x, 0, ny // 4)
        e_rows(x, ny - ny // 4, ny // 4)
        return carry

    lax.fori_loop(1, last_x, middle_rows, 0, unroll=2)

    sent_yz.wait()
    sent_ye.wait()
    sent_yp.wait()

    @pl.when(jnp.logical_not(low))
    def _():
        bottom = lax.broadcasted_iota(jnp.int32, (8, nz), 0) == 7
        missing = jnp.where(bottom, COURANT * yz[nx : nx + 8, :], 0.0)
        for r, c, x, k in places:
            if c == 0:
                edge = pltpu.roll(missing, nz - k, 1) if k else missing
                below[r, 0, x, ny - 8 : ny, :] = below[r, 0, x, ny - 8 : ny, :] - edge

    for r in range(2):
        h0, h2 = hbuf[r, 0, 1:nx, ny + 7, :], hbuf[r, 2, 1:nx, ny + 7, :]
        hbuf[r, 0, 1:nx, ny + 7, :] = h0 - COURANT * ye[r, 1, 0:last_x]
        hbuf[r, 2, 1:nx, ny + 7, :] = h2 + COURANT * ye[r, 0, 0:last_x]
        edge = pltpu.roll(yz[0:nx, :], nz - 1 - r, 1)
        edge = jnp.where(lane_x == nz - 1, half_low * edge, 0.0)
        hbuf[r, 0, 1 : nx + 1, 7, :] = yp[r, 0] - COURANT * ye_out[r, 1] + edge
        hbuf[r, 2, 1 : nx + 1, 7, :] = yp[r, 1] + COURANT * ye_out[r, 0]

    lax.fori_loop(1, last_x, outer_rows, 0, unroll=2)

    sent_xe.wait()
    sent_xp.wait()
    sent_xz.wait()
    sent_xya.wait()
    sent_xyb.wait()

    @pl.when(low)
    def _():
        for r, c, x, k in places:
            if x == last_x:
                add_above(r, c, x, k)

    for r in range(2):
        row_0, row_2 = hbuf[r, 0, nx, ny + 7 : ny + 8, :], hbuf[r, 2, nx, ny + 7 : ny + 8, :]
        hbuf[r, 0, nx, ny + 7 : ny + 8, :] = row_0 - COURANT * ye[r, 1, last_x:nx, :]
        hbuf[r, 2, nx, ny + 7 : ny + 8, :] = row_2 + COURANT * ye[r, 0, last_x:nx, :]
        hbuf[r, 2, nx, 7:8, :] = hbuf[r, 2, nx, 7:8, :] - COURANT * xyb[r : r + 1, :]
        hbuf[r, 1, nx, 8 : ny + 8, :] = hbuf[r, 1, nx, 8 : ny + 8, :] + COURANT * xe[r, 1]
        hbuf[r, 2, nx, 8 : ny + 8, :] = hbuf[r, 2, nx, 8 : ny + 8, :] - COURANT * xe[r, 0]
        k = r * 2 * nx + 2 * nx - 1
        column = pltpu.roll(xz[...], nz - k, 1)
        below[r, 1, last_x] = below[r, 1, last_x] + half_high * column
        edge = jnp.where(lane == nz - 1, half_low * pltpu.roll(column, nz - 1, 1), 0.0)
        hbuf[r, 1, 0, 8 : ny + 8, :] = xp[r, 0] + COURANT * ebuf[r, 2, 0, 0:ny, :] - edge
        corner = jnp.where(row == ny - 1, COURANT * xya[r : r + 1, :], 0.0)
        hbuf[r, 2, 0, 8 : ny + 8, :] = xp[r, 1] - COURANT * ebuf[r, 1, 0, 0:ny, :] + corner

    e_rows(0, 0, ny)
    e_rows(last_x, 0, ny)

    sums = lax.dot_general(
        onehot, prod[...], (((1,), (1,)), ((), ())),
        precision=lax.Precision.HIGHEST, preferred_element_type=F32,
    )
    part_out[...] = jnp.where(low, sums[owned:LAYERS], sums[0:owned])
    last = send(9, part_out, part_in, to_z)
    mine = jnp.where(low, sums[0:owned], sums[owned:LAYERS])
    last.wait()
    result = (mine + part_in[...]) / own_thickness
    for x in range(nx):
        grad[:, x, :] = result[:, x * ny : (x + 1) * ny]


def store_kernel(ebuf, hbuf, grad, oef, ohf, oea, oha, ograd, sem):
    nx, ny = oef.shape[1:3]
    copies = [
        pltpu.make_async_copy(ebuf.at[0, :, 0:nx, 0:ny, :], oef, sem.at[0]),
        pltpu.make_async_copy(hbuf.at[0, :, 1 : nx + 1, 8 : ny + 8, :], ohf, sem.at[1]),
        pltpu.make_async_copy(ebuf.at[1, :, 0:nx, 0:ny, :], oea, sem.at[2]),
        pltpu.make_async_copy(hbuf.at[1, :, 1 : nx + 1, 8 : ny + 8, :], oha, sem.at[3]),
        pltpu.make_async_copy(grad, ograd, sem.at[4]),
    ]
    for copy in copies:
        copy.start()
    for copy in copies:
        copy.wait()


def shards(ef, hf, ea, ha, mat, df, da, freq, lmap):
    comps, nx, ny, nz = ef.shape
    freqs, _, _, slab = df.shape[:4]
    df = jnp.transpose(df, (0, 1, 2, 4, 5, 3))
    da = jnp.transpose(da, (0, 1, 2, 4, 5, 3))
    args = [pltpu.with_memory_space_constraint(a, pltpu.HBM) for a in (ef, hf, ea, ha, mat, df, da, freq, lmap)]
    hbm = pl.BlockSpec(memory_space=pltpu.HBM)
    vmem = pl.BlockSpec(memory_space=pltpu.VMEM)
    padded = (2, comps, nx + 1, ny + 8, nz)
    owned = LAYERS // 2
    out = pl.pallas_call(
        step_kernel,
        name="yee_step",
        out_shape=(
            pltpu.VMEM(padded, F32),
            pltpu.VMEM(padded, F32),
            pltpu.VMEM((owned, nx, ny), F32),
        ),
        in_specs=[hbm] * 9,
        out_specs=[vmem] * 3,
        scratch_shapes=[
            pltpu.VMEM((nx, ny, nz), jnp.int32),
            pltpu.VMEM(df.shape, F32),
            pltpu.VMEM(da.shape, F32),
            pltpu.SMEM(freq.shape, F32),
            pltpu.VMEM(lmap.shape, jnp.int32),
            pltpu.VMEM((comps, nx, ny, nz), F32),
            pltpu.VMEM((comps, nx, ny, nz), F32),
            pltpu.VMEM((nx, ny, nz), F32),
            pltpu.VMEM((nx * ny, nz), F32),
            pltpu.VMEM((2, 2, nx, ny, nz), F32),
            pltpu.VMEM((2, 2, nx, nz), F32),
            pltpu.VMEM((2, nz), F32),
            pltpu.VMEM((2, nz), F32),
            pltpu.VMEM((ny, nz), F32),
            pltpu.VMEM((nx + 8, nz), F32),
            pltpu.VMEM((2, 2, nx, nz), F32),
            pltpu.VMEM((ny, nz), F32),
            pltpu.VMEM((owned, nx * ny), F32),
            pltpu.VMEM((2, 2, ny, nz), F32),
            pltpu.VMEM((2, 2, nx, nz), F32),
            pltpu.VMEM((2, nz), F32),
            pltpu.VMEM((2, nz), F32),
            pltpu.VMEM((ny, nz), F32),
            pltpu.VMEM((nx + 8, nz), F32),
            pltpu.VMEM((2, 2, ny, nz), F32),
            pltpu.VMEM((2, 2, nx, nz), F32),
            pltpu.VMEM((ny, nz), F32),
            pltpu.VMEM((owned, nx * ny), F32),
            pltpu.SemaphoreType.DMA((4, QUARTERS)),
            pltpu.SemaphoreType.DMA((3,)),
            pltpu.SemaphoreType.DMA((2, QUARTERS)),
            pltpu.SemaphoreType.DMA((10,)),
            pltpu.SemaphoreType.DMA((10,)),
        ],
        compiler_params=pltpu.CompilerParams(
            collective_id=0, has_side_effects=True, vmem_limit_bytes=24 << 20
        ),
    )(*args)
    staged = [pltpu.with_memory_space_constraint(o, pltpu.VMEM) for o in out]
    field = jax.ShapeDtypeStruct(ef.shape, F32)
    return pl.pallas_call(
        store_kernel,
        name="store_fields",
        out_shape=(field, field, field, field, jax.ShapeDtypeStruct((owned, nx, ny), F32)),
        in_specs=[vmem] * 3,
        out_specs=[hbm] * 5,
        scratch_shapes=[pltpu.SemaphoreType.DMA((5,))],
        compiler_params=pltpu.CompilerParams(vmem_limit_bytes=1 << 20),
    )(*staged)


def solution(mesh):
    field = P(None, "gx", "gy", "gz")
    dft = P(None, None, None, "gz", "gx", "gy")
    in_specs = (field, field, field, field, P("gx", "gy", "gz"), dft, dft, P(), P())
    out_specs = (field, field, field, field, P("gz", "gx", "gy"))
    return jax.shard_map(shards, mesh=mesh, in_specs=in_specs, out_specs=out_specs, check_vma=False)
```

```python
import jax
import jax.numpy as jnp
from jax import lax
from jax.experimental import pallas as pl
from jax.experimental.pallas import tpu as pltpu
from jax.sharding import PartitionSpec as P

LAYERS = 16
STEP = 40
COURANT = 0.5
PERMITTIVITIES = (1.0, 2.1, 4.0, 12.0)
MESH = pl.DeviceIdType.MESH
F32 = jnp.float32
QUARTERS = 4


def step_kernel(
    ef, hf, ea, ha, mat, df, da, freq, lmap,
    ebuf, hbuf, grad,
    matb, dfb, dab, freqb, lmapb, ubuf, vbuf, gbuf, prod, below,
    ye_out, xya_out, xyb_out, xz_out, yz_out, yp_out, z_out, part_out,
    xe, ye, xya, xyb, xz, yz, xp, yp, zf, part_in,
    fsem, lsem, dsem, ssem, rsem,
):
    nx, ny, nz = mat.shape
    freqs, slab = df.shape[0], df.shape[5]
    owned = LAYERS // 2
    gx, gy, gz = lax.axis_index("gx"), lax.axis_index("gy"), lax.axis_index("gz")
    sx, sy = lax.axis_size("gx"), lax.axis_size("gy")
    x_up, x_down = lax.rem(gx + 1, sx), lax.rem(gx + sx - 1, sx)
    y_up, y_down = lax.rem(gy + 1, sy), lax.rem(gy + sy - 1, sy)
    z_other = 1 - gz
    low = gz == 0
    x_cross = lax.rem(gx + sx + 2 * gz - 1, sx)
    y_cross = lax.rem(gy + sy + 2 * gz - 1, sy)

    to_xe, to_xp = {"gx": x_down}, {"gx": x_up}
    to_ye, to_yp = {"gy": y_down}, {"gy": y_up}
    to_z = {"gz": z_other}
    to_xya, to_xyb = {"gx": x_up, "gy": y_down}, {"gx": x_down, "gy": y_up}
    to_xz, to_yz = {"gx": x_cross, "gz": z_other}, {"gy": y_cross, "gz": z_other}
    peers = (to_xe, to_xp, to_ye, to_yp, to_z, to_xya, to_xyb, to_xz, to_yz)
    barrier = pltpu.get_barrier_semaphore()
    for peer in peers:
        pl.semaphore_signal(barrier, inc=1, device_id=peer, device_id_type=MESH)

    rows = nx // QUARTERS
    field_loads = []
    for q in reversed(range(QUARTERS)):
        part, inner = pl.ds(q * rows, rows), pl.ds(q * rows + 1, rows)
        group = [
            pltpu.make_async_copy(ef.at[:, part], ebuf.at[0, :, part, 0:ny, :], fsem.at[0, q]),
            pltpu.make_async_copy(ea.at[:, part], ebuf.at[1, :, part, 0:ny, :], fsem.at[1, q]),
            pltpu.make_async_copy(hf.at[:, part], hbuf.at[0, :, inner, 8 : ny + 8, :], fsem.at[2, q]),
            pltpu.make_async_copy(ha.at[:, part], hbuf.at[1, :, inner, 8 : ny + 8, :], fsem.at[3, q]),
        ]
        for load in group:
            load.start()
        field_loads.append((q, group))
    loads = [
        pltpu.make_async_copy(freq, freqb, lsem.at[0]),
        pltpu.make_async_copy(lmap, lmapb, lsem.at[1]),
        pltpu.make_async_copy(mat, matb, lsem.at[2]),
    ]
    for load in loads:
        load.start()
    dft_loads = []
    for q in range(QUARTERS):
        part = pl.ds(q * rows, rows)
        pair = (
            pltpu.make_async_copy(df.at[:, :, :, part], dfb.at[:, :, :, part], dsem.at[0, q]),
            pltpu.make_async_copy(da.at[:, :, :, part], dab.at[:, :, :, part], dsem.at[1, q]),
        )
        dft_loads.append(pair)
    for pair in dft_loads[:2]:
        for load in pair:
            load.start()

    lane = lax.broadcasted_iota(jnp.int32, (ny, nz), 1)
    row = lax.broadcasted_iota(jnp.int32, (ny, nz), 0)
    lane_x = lax.broadcasted_iota(jnp.int32, (nx, nz), 1)
    row_x = lax.broadcasted_iota(jnp.int32, (nx, nz), 0)

    def copy_to(index, src, dst, peer):
        return pltpu.make_async_remote_copy(
            src_ref=src, dst_ref=dst, send_sem=ssem.at[index], recv_sem=rsem.at[index],
            device_id=peer, device_id_type=MESH,
        )

    def send(index, src, dst, peer):
        copy = copy_to(index, src, dst, peer)
        copy.start()
        return copy

    def gather_lane(tile_of, from_lane, first):
        acc = z_out[...]
        for k in range(4 * nx):
            if first <= k % nx < first + rows:
                tile = tile_of(k // (2 * nx), k // nx % 2, k % nx)
                by = (k - from_lane) % nz
                acc = jnp.where(lane == k, pltpu.roll(tile, by, 1) if by else tile, acc)
        z_out[...] = acc

    zero_row = jnp.zeros((nx, nz), F32)
    for r in range(2):
        ebuf[r, 0, 0:nx, ny, :] = zero_row
        ebuf[r, 2, 0:nx, ny, :] = zero_row
    z_out[...] = jnp.zeros_like(z_out)

    def h_plane(x, last=False):
        for r in range(2):
            e0 = ebuf[r, 0, x, 0:ny, :]
            e1 = ebuf[r, 1, x, 0:ny, :]
            e2 = ebuf[r, 2, x, 0:ny, :]

            def up_z(value):
                return jnp.where(lane == nz - 1, 0.0, pltpu.roll(value, nz - 1, 1))

            curl_x = (ebuf[r, 2, x, 1 : ny + 1, :] - e2) - (up_z(e1) - e1)
            curl_y = up_z(e0) - e0
            curl_z = ebuf[r, 0, x, 1 : ny + 1, :] - e0
            if last:
                curl_y = curl_y + e2
                curl_z = -e1 - curl_z
            else:
                curl_y = curl_y - (ebuf[r, 2, x + 1, 0:ny, :] - e2)
                curl_z = (ebuf[r, 1, x + 1, 0:ny, :] - e1) - curl_z
            for c, curl in enumerate((curl_x, curl_y, curl_z)):
                hbuf[r, c, x + 1, 8 : ny + 8, :] = hbuf[r, c, x + 1, 8 : ny + 8, :] - COURANT * curl

    def h_body(x, carry):
        h_plane(x)
        return carry

    for q, group in field_loads:
        for load in group:
            load.wait()
        if q == QUARTERS - 1:
            h_plane(nx - 1, last=True)
        lax.fori_loop(q * rows, min((q + 1) * rows, nx - 1), h_body, 0, unroll=True)

        @pl.when(low)
        def _():
            gather_lane(lambda r, c, x: hbuf[r, c, x + 1, 8 : ny + 8, :], nz - 1, q * rows)

        @pl.when(jnp.logical_not(low))
        def _():
            gather_lane(lambda r, c, x: ebuf[r, 1 - c, x, 0:ny, :], 0, q * rows)

    for r in range(2):
        for i, c in enumerate((0, 2)):
            yp_out[r, i] = hbuf[r, c, 1 : nx + 1, ny + 7, :]

    xz_tile = jnp.zeros((ny, nz), F32)
    yz_tile = jnp.zeros((nx, nz), F32)
    yz_row = jnp.zeros((1, nz), F32)
    for r in range(2):
        for i, c in enumerate((0, 2)):
            ye_out[r, i] = ebuf[r, c, 0:nx, 0, :]
        xya_out[r : r + 1, :] = ebuf[r, 0, nx - 1, 0:1, :]
        xyb_out[r : r + 1, :] = ebuf[r, 1, 0, ny - 1 : ny, :]
        k = r * 2 * nx + 2 * nx - 1
        column = jnp.where(
            low, pltpu.roll(ebuf[r, 2, 0, 0:ny, :], k + 1, 1), pltpu.roll(ebuf[r, 0, nx - 1, 0:ny, :], k, 1)
        )
        xz_tile = jnp.where(lane == k, column, xz_tile)
        column = ebuf[r, 1, 0:nx, ny - 1, :]
        yz_tile = jnp.where(lane_x == r, column if r == 0 else pltpu.roll(column, r, 1), yz_tile)
        column = jnp.broadcast_to(ye_out[r, 1][:, nz - 1 : nz], (nx, nz))
        picked = jnp.where(lane_x == r * 2 * nx + row_x, column, 0.0)
        yz_row = yz_row + jnp.sum(picked, axis=0, keepdims=True)
    xz_out[...] = xz_tile
    yz_out[0:nx, :] = yz_tile
    yz_out[nx : nx + 8, :] = jnp.broadcast_to(yz_row, (8, nz))

    pl.semaphore_wait(barrier, len(peers))
    sent_xya = send(0, xya_out, xya, to_xya)
    sent_xyb = send(1, xyb_out, xyb, to_xyb)
    sent_xz = send(4, xz_out, xz, to_xz)
    sent_yz = send(5, yz_out, yz, to_yz)
    sent_z = send(8, z_out, zf, to_z)
    sent_yp = send(7, yp_out, yp, to_yp)
    sent_ye = send(2, ye_out, ye, to_ye)
    sent_xp = send(6, hbuf.at[:, 1:3, nx, 8 : ny + 8, :], xp, to_xp)
    sent_xe = send(3, ebuf.at[:, 1:3, 0, 0:ny, :], xe, to_xe)
    for pair in dft_loads[2:]:
        for load in pair:
            load.start()
    below[...] = jnp.zeros_like(below)
    loads[0].wait()
    loads[1].wait()
    cosine, sine = [], []
    squares = None
    for f in range(freqs):
        phase = jnp.full((8, nz), freqb[f] * STEP, F32)
        cos_f, sin_f = jnp.cos(phase)[0:1], jnp.sin(phase)[0:1]
        cosine.append(cos_f[:, 0:slab])
        sine.append(sin_f[:, 0:slab])
        term = cos_f * cos_f - sin_f * sin_f
        squares = term if squares is None else squares + term
    shift = (nz - slab) * z_other
    layer_map = lmapb[...].reshape(1, 2 * slab)
    layer_ids = lax.broadcasted_iota(jnp.int32, (LAYERS, 2 * slab), 0)
    onehot_all = (layer_map == layer_ids).astype(F32)
    thickness = jnp.sum(onehot_all, axis=1, keepdims=True)
    own_thickness = 3.0 * jnp.where(low, thickness[0:owned], thickness[owned:LAYERS])

    def place(value):
        rest = jnp.zeros((value.shape[0], nz - slab), F32)
        return pltpu.roll(jnp.concatenate([value, rest], axis=1), shift, 1)

    onehot = place(jnp.where(low, onehot_all[:, 0:slab], onehot_all[:, slab : 2 * slab]))

    def dft_plane(x, carry):
        total = None
        for c in range(3):
            u = v = None
            for f in range(freqs):
                rf, mf = dfb[f, 0, c, x], dfb[f, 1, c, x]
                ra, ma = dab[f, 0, c, x], dab[f, 1, c, x]
                base = rf * ra - mf * ma
                total = base if total is None else total + base
                u_f = cosine[f] * ra + sine[f] * ma
                v_f = cosine[f] * rf + sine[f] * mf
                u = u_f if u is None else u + u_f
                v = v_f if v is None else v + v_f
            ubuf[c, x] = place(u)
            vbuf[c, x] = place(v)
        gbuf[x] = place(total)
        return carry

    for q in range(QUARTERS):
        for load in dft_loads[q]:
            load.wait()
        lax.fori_loop(q * rows, (q + 1) * rows, dft_plane, 0, unroll=2)
    loads[2].wait()

    half_low = jnp.where(low, COURANT, 0.0)
    half_high = COURANT - half_low
    sent_z.wait()
    z_sign = jnp.where(lax.rem(lax.div(lane, nx), 2) == 0, COURANT, -COURANT)
    places = [(r, c, x, (r * 2 + c) * nx + x) for r in range(2) for c in range(2) for x in range(nx)]
    last_x = nx - 1

    def add_above(r, c, x, k):
        edge = jnp.where(lane == nz - 1, pltpu.roll(z_sign * zf[...], nz - 1 - k, 1), 0.0)
        hbuf[r, c, x + 1, 8 : ny + 8, :] = hbuf[r, c, x + 1, 8 : ny + 8, :] + edge

    @pl.when(low)
    def _():
        for r, c, x, k in places:
            if x < last_x:
                add_above(r, c, x, k)

    @pl.when(jnp.logical_not(low))
    def _():
        z_below = zf[...] + z_sign * z_out[...]
        for r, c, x, k in places:
            below[r, c, x] = pltpu.roll(z_below, nz - k, 1) if k else z_below

    def e_rows(x, y0, n):
        own, ahead = pl.ds(y0 + 8, n), pl.ds(y0 + 7, n)
        cell = pl.ds(y0, n)
        first_lane = lane[0:n] == 0
        m = matb[x, cell]
        coefficient = jnp.where(
            m == 0, COURANT / PERMITTIVITIES[0],
            jnp.where(m == 1, COURANT / PERMITTIVITIES[1],
                      jnp.where(m == 2, COURANT / PERMITTIVITIES[2], COURANT / PERMITTIVITIES[3])),
        ).astype(F32)
        cells = []
        for r in range(2):
            h0 = hbuf[r, 0, x + 1, own, :]
            h1 = hbuf[r, 1, x + 1, own, :]
            h2 = hbuf[r, 2, x + 1, own, :]

            def down_z(value, c):
                return jnp.where(first_lane, below[r, c, x, cell], pltpu.roll(value, 1, 1))

            curl_x = (h2 - hbuf[r, 2, x + 1, ahead, :]) - (h1 - down_z(h1, 1))
            curl_y = (h0 - down_z(h0, 0)) - (h2 - hbuf[r, 2, x, own, :])
            curl_z = (h1 - hbuf[r, 1, x, own, :]) - (h0 - hbuf[r, 0, x + 1, ahead, :])
            fields = []
            for c, curl in enumerate((curl_x, curl_y, curl_z)):
                new_e = ebuf[r, c, x, cell, :] + coefficient * curl
                ebuf[r, c, x, cell, :] = new_e
                fields.append(new_e)
            cells.append(fields)
        total = gbuf[x, cell]
        for c in range(3):
            fwd, adj = cells[0][c], cells[1][c]
            total = total + (fwd * (ubuf[c, x, cell] + squares * adj) + adj * vbuf[c, x, cell])
        start = x * ny + y0
        prod[pl.ds(start if isinstance(x, int) else pl.multiple_of(start, 8), n), :] = total

    half = ny // 2

    def middle_rows(x, carry):
        e_rows(x, ny // 4, half)
        return carry

    def outer_rows(x, carry):
        e_rows(x, 0, ny // 4)
        e_rows(x, ny - ny // 4, ny // 4)
        return carry

    lax.fori_loop(1, last_x, middle_rows, 0, unroll=7)

    sent_yz.wait()
    sent_ye.wait()
    sent_yp.wait()

    @pl.when(jnp.logical_not(low))
    def _():
        bottom = lax.broadcasted_iota(jnp.int32, (8, nz), 0) == 7
        missing = jnp.where(bottom, COURANT * yz[nx : nx + 8, :], 0.0)
        for r, c, x, k in places:
            if c == 0:
                edge = pltpu.roll(missing, nz - k, 1) if k else missing
                below[r, 0, x, ny - 8 : ny, :] = below[r, 0, x, ny - 8 : ny, :] - edge

    for r in range(2):
        h0, h2 = hbuf[r, 0, 1:nx, ny + 7, :], hbuf[r, 2, 1:nx, ny + 7, :]
        hbuf[r, 0, 1:nx, ny + 7, :] = h0 - COURANT * ye[r, 1, 0:last_x]
        hbuf[r, 2, 1:nx, ny + 7, :] = h2 + COURANT * ye[r, 0, 0:last_x]
        edge = pltpu.roll(yz[0:nx, :], nz - 1 - r, 1)
        edge = jnp.where(lane_x == nz - 1, half_low * edge, 0.0)
        hbuf[r, 0, 1 : nx + 1, 7, :] = yp[r, 0] - COURANT * ye_out[r, 1] + edge
        hbuf[r, 2, 1 : nx + 1, 7, :] = yp[r, 1] + COURANT * ye_out[r, 0]

    lax.fori_loop(1, last_x, outer_rows, 0, unroll=7)

    sent_xe.wait()
    sent_xp.wait()
    sent_xz.wait()
    sent_xya.wait()
    sent_xyb.wait()

    @pl.when(low)
    def _():
        for r, c, x, k in places:
            if x == last_x:
                add_above(r, c, x, k)

    for r in range(2):
        row_0, row_2 = hbuf[r, 0, nx, ny + 7 : ny + 8, :], hbuf[r, 2, nx, ny + 7 : ny + 8, :]
        hbuf[r, 0, nx, ny + 7 : ny + 8, :] = row_0 - COURANT * ye[r, 1, last_x:nx, :]
        hbuf[r, 2, nx, ny + 7 : ny + 8, :] = row_2 + COURANT * ye[r, 0, last_x:nx, :]
        hbuf[r, 2, nx, 7:8, :] = hbuf[r, 2, nx, 7:8, :] - COURANT * xyb[r : r + 1, :]
        hbuf[r, 1, nx, 8 : ny + 8, :] = hbuf[r, 1, nx, 8 : ny + 8, :] + COURANT * xe[r, 1]
        hbuf[r, 2, nx, 8 : ny + 8, :] = hbuf[r, 2, nx, 8 : ny + 8, :] - COURANT * xe[r, 0]
        k = r * 2 * nx + 2 * nx - 1
        column = pltpu.roll(xz[...], nz - k, 1)
        below[r, 1, last_x] = below[r, 1, last_x] + half_high * column
        edge = jnp.where(lane == nz - 1, half_low * pltpu.roll(column, nz - 1, 1), 0.0)
        hbuf[r, 1, 0, 8 : ny + 8, :] = xp[r, 0] + COURANT * ebuf[r, 2, 0, 0:ny, :] - edge
        corner = jnp.where(row == ny - 1, COURANT * xya[r : r + 1, :], 0.0)
        hbuf[r, 2, 0, 8 : ny + 8, :] = xp[r, 1] - COURANT * ebuf[r, 1, 0, 0:ny, :] + corner

    e_rows(0, 0, ny)
    e_rows(last_x, 0, ny)

    sums = lax.dot_general(
        onehot, prod[...], (((1,), (1,)), ((), ())),
        precision=lax.Precision.HIGHEST, preferred_element_type=F32,
    )
    part_out[...] = jnp.where(low, sums[owned:LAYERS], sums[0:owned])
    last = send(9, part_out, part_in, to_z)
    mine = jnp.where(low, sums[0:owned], sums[owned:LAYERS])
    last.wait()
    result = (mine + part_in[...]) / own_thickness
    for x in range(nx):
        grad[:, x, :] = result[:, x * ny : (x + 1) * ny]


def store_kernel(ebuf, hbuf, grad, oef, ohf, oea, oha, ograd, sem):
    nx, ny = oef.shape[1:3]
    copies = [
        pltpu.make_async_copy(ebuf.at[0, :, 0:nx, 0:ny, :], oef, sem.at[0]),
        pltpu.make_async_copy(hbuf.at[0, :, 1 : nx + 1, 8 : ny + 8, :], ohf, sem.at[1]),
        pltpu.make_async_copy(ebuf.at[1, :, 0:nx, 0:ny, :], oea, sem.at[2]),
        pltpu.make_async_copy(hbuf.at[1, :, 1 : nx + 1, 8 : ny + 8, :], oha, sem.at[3]),
        pltpu.make_async_copy(grad, ograd, sem.at[4]),
    ]
    for copy in copies:
        copy.start()
    for copy in copies:
        copy.wait()


def shards(ef, hf, ea, ha, mat, df, da, freq, lmap):
    comps, nx, ny, nz = ef.shape
    freqs, _, _, slab = df.shape[:4]
    df = jnp.transpose(df, (0, 1, 2, 4, 5, 3))
    da = jnp.transpose(da, (0, 1, 2, 4, 5, 3))
    args = [pltpu.with_memory_space_constraint(a, pltpu.HBM) for a in (ef, hf, ea, ha, mat, df, da, freq, lmap)]
    hbm = pl.BlockSpec(memory_space=pltpu.HBM)
    vmem = pl.BlockSpec(memory_space=pltpu.VMEM)
    padded = (2, comps, nx + 1, ny + 8, nz)
    owned = LAYERS // 2
    out = pl.pallas_call(
        step_kernel,
        name="yee_step",
        out_shape=(
            pltpu.VMEM(padded, F32),
            pltpu.VMEM(padded, F32),
            pltpu.VMEM((owned, nx, ny), F32),
        ),
        in_specs=[hbm] * 9,
        out_specs=[vmem] * 3,
        scratch_shapes=[
            pltpu.VMEM((nx, ny, nz), jnp.int32),
            pltpu.VMEM(df.shape, F32),
            pltpu.VMEM(da.shape, F32),
            pltpu.SMEM(freq.shape, F32),
            pltpu.VMEM(lmap.shape, jnp.int32),
            pltpu.VMEM((comps, nx, ny, nz), F32),
            pltpu.VMEM((comps, nx, ny, nz), F32),
            pltpu.VMEM((nx, ny, nz), F32),
            pltpu.VMEM((nx * ny, nz), F32),
            pltpu.VMEM((2, 2, nx, ny, nz), F32),
            pltpu.VMEM((2, 2, nx, nz), F32),
            pltpu.VMEM((2, nz), F32),
            pltpu.VMEM((2, nz), F32),
            pltpu.VMEM((ny, nz), F32),
            pltpu.VMEM((nx + 8, nz), F32),
            pltpu.VMEM((2, 2, nx, nz), F32),
            pltpu.VMEM((ny, nz), F32),
            pltpu.VMEM((owned, nx * ny), F32),
            pltpu.VMEM((2, 2, ny, nz), F32),
            pltpu.VMEM((2, 2, nx, nz), F32),
            pltpu.VMEM((2, nz), F32),
            pltpu.VMEM((2, nz), F32),
            pltpu.VMEM((ny, nz), F32),
            pltpu.VMEM((nx + 8, nz), F32),
            pltpu.VMEM((2, 2, ny, nz), F32),
            pltpu.VMEM((2, 2, nx, nz), F32),
            pltpu.VMEM((ny, nz), F32),
            pltpu.VMEM((owned, nx * ny), F32),
            pltpu.SemaphoreType.DMA((4, QUARTERS)),
            pltpu.SemaphoreType.DMA((3,)),
            pltpu.SemaphoreType.DMA((2, QUARTERS)),
            pltpu.SemaphoreType.DMA((10,)),
            pltpu.SemaphoreType.DMA((10,)),
        ],
        compiler_params=pltpu.CompilerParams(
            collective_id=0, has_side_effects=True, vmem_limit_bytes=24 << 20
        ),
    )(*args)
    staged = [pltpu.with_memory_space_constraint(o, pltpu.VMEM) for o in out]
    field = jax.ShapeDtypeStruct(ef.shape, F32)
    return pl.pallas_call(
        store_kernel,
        name="store_fields",
        out_shape=(field, field, field, field, jax.ShapeDtypeStruct((owned, nx, ny), F32)),
        in_specs=[vmem] * 3,
        out_specs=[hbm] * 5,
        scratch_shapes=[pltpu.SemaphoreType.DMA((5,))],
        compiler_params=pltpu.CompilerParams(vmem_limit_bytes=1 << 20),
    )(*staged)


def solution(mesh):
    field = P(None, "gx", "gy", "gz")
    dft = P(None, None, None, "gz", "gx", "gy")
    in_specs = (field, field, field, field, P("gx", "gy", "gz"), dft, dft, P(), P())
    out_specs = (field, field, field, field, P("gz", "gx", "gy"))
    return jax.shard_map(shards, mesh=mesh, in_specs=in_specs, out_specs=out_specs, check_vma=False)
```
